32 devices in a mesh: section: 2 (over y), dp: 16 (over z, x, core).
Axes of the slice: x: 2, y: 2, z: 4, core: 2. Of those that a mesh axis runs over, the one named last changes fastest.
Arguments:
- token_ids: int32 [32, 128], P('dp'), may hold values from 0 to 4095
- target_ids: int32 [32, 128], P('dp'), may hold values from 0 to 4095
- segment_ids: int32 [32, 128], P('dp'), may hold values from 0 to 3, never falling along the last dimension, each value on 1 to 64 neighbouring positions
- token_embed: bfloat16 [4096, 768], P('dp'), may hold values from -0.41992188 to 0.41992188
- pos_embed: bfloat16 [1024, 768], replicated, may hold values from -0.59765625 to 0.59765625
- final_gain: bfloat16 [768], replicated, may hold values from 0.5 to 1.5
- final_bias: bfloat16 [768], replicated, may hold values from -1 to 1
- ln1_gain: bfloat16 [2, 768], P('section'), may hold values from 0.5 to 1.5
- ln1_bias: bfloat16 [2, 768], P('section'), may hold values from -1 to 1
- qkv_weight: bfloat16 [2, 768, 2304], P('section'), may hold values from -0.21875 to 0.21875
- qv_bias: bfloat16 [2, 1536], P('section'), may hold values from -1 to 1
- out_weight: bfloat16 [2, 768, 768], P('section'), may hold values from -0.625 to 0.625
- out_bias: bfloat16 [2, 768], P('section'), may hold values from -1 to 1
- ln2_gain: bfloat16 [2, 768], P('section'), may hold values from 0.5 to 1.5
- ln2_bias: bfloat16 [2, 768], P('section'), may hold values from -1 to 1
- fc_weight: bfloat16 [2, 768, 3072], P('section'), may hold values from -0.21875 to 0.21875
- fc_bias: bfloat16 [2, 3072], P('section'), may hold values from -1 to 1
- proj_weight: bfloat16 [2, 3072, 768], P('section'), may hold values from -0.109375 to 0.109375
- proj_bias: bfloat16 [2, 768], P('section'), may hold values from -1 to 1
Outputs:
- loss: float32 [], replicated
- grad_token_embed: float32 [4096, 768], P('dp')
- grad_pos_embed: float32 [1024, 768], P('dp')
- grad_final_gain: float32 [768], P('dp')
- grad_final_bias: float32 [768], P('dp')
- grad_ln1_gain: float32 [2, 768], P('section', 'dp')
- grad_ln1_bias: float32 [2, 768], P('section', 'dp')
- grad_qkv_weight: float32 [2, 768, 2304], P('section', 'dp')
- grad_qv_bias: float32 [2, 1536], P('section', 'dp')
- grad_out_weight: float32 [2, 768, 768], P('section', 'dp')
- grad_out_bias: float32 [2, 768], P('section', 'dp')
- grad_ln2_gain: float32 [2, 768], P('section', 'dp')
- grad_ln2_bias: float32 [2, 768], P('section', 'dp')
- grad_fc_weight: float32 [2, 768, 3072], P('section', 'dp')
- grad_fc_bias: float32 [2, 3072], P('section', 'dp')
- grad_proj_weight: float32 [2, 3072, 768], P('section', 'dp')
- grad_proj_bias: float32 [2, 768], P('section', 'dp')
The draws below stay inside these ranges and needn't reach their ends.
Inputs may be any that keep to these rules, and one draw needn't show every extreme that they name: `segment_ids`: segment numbers never fall along a row; each segment holds 1 to 64 positions.
All inputs are finite; a program needn't handle non-finite values.
Results may differ from the reference program's by a relative error of at most 0.0035.
Values may be sent and summed in bfloat16 or wider, within the bound.
No kernel may reach another device: no remote copies, remote signals or barrier semaphores. Data moves between devices by JAX's collectives and lax.ppermute only.
A program may use at most 512 MiB of HBM per device.

```python
import math
import jax
import jax.numpy as jnp
import numpy as np
from jax import lax

D = 768
HEADS = 12
HD = 64
FF = 3072
POS = 1024
LEN = 128
VOCAB = 4096
BATCH = 32
N_SECTION = 2


def place_ends(array, key, smallest, largest):
    index_at = [jax.random.randint(jax.random.fold_in(key, axis), (), 0, length) for axis, length in enumerate(array.shape)]
    widest = array.shape.index(max(array.shape))
    beside = index_at[:widest] + [(index_at[widest] + 1) % array.shape[widest]] + index_at[widest + 1:]
    return array.at[tuple(index_at)].set(smallest).at[tuple(beside)].set(largest)


def shard_levels(key, extent, cuts, low, top_value):
    level = 1.0
    for dim, shards_of in cuts:
        draws = jax.random.uniform(jax.random.fold_in(jax.random.fold_in(key, 6), dim), (shards_of,), jnp.float32, low / len(cuts), top_value / len(cuts))
        level = level * jnp.repeat(jnp.exp(draws), extent[dim] // shards_of).reshape((-1,) + (1,) * (len(extent) - 1 - dim))
    return level


def rank_bounds(amount, skew):
    weights = [(1 << 20) // math.isqrt(rank ** skew) + 1 for rank in range(1, amount + 1)]
    scale = 1 + sum(weights) // (1 << 30)
    return np.cumsum(np.array([max(1, weight // scale) for weight in weights]))


def ranked_ids(rng, dims, number_of, slope):
    grid = rank_bounds(number_of, slope)
    ticket = jax.random.randint(jax.random.fold_in(rng, 1), dims, 0, int(grid[number_of - 1]))
    rank = jnp.searchsorted(jnp.asarray(grid, jnp.int32), ticket, side="right")
    return jax.random.permutation(jax.random.fold_in(rng, 2), number_of)[rank].astype(jnp.int32)


def profile(amount, total, limit, slope):
    portions = [(1 << 20) // math.isqrt(standing ** slope) + 1 for standing in range(2, amount + 1)]
    rest, counts = total - limit - (amount - 1), [1] * (amount - 1)
    while rest > 0:
        free = [i for i in range(amount - 1) if counts[i] < limit]
        mass, left = sum([portions[i] for i in free]), rest
        for i in free:
            extra = min(limit - counts[i], max(1, left * portions[i] // mass), rest)
            counts[i] = counts[i] + extra
            rest = rest - extra
    return np.array([limit] + counts)


def ragged(stream_key, count, total, bound, slope):
    if count == 2:
        one = jax.random.randint(stream_key, (), max(1, total - bound), min(bound, total - 1) + 1)
        return jnp.stack([one, total - one])
    lengths = jnp.asarray(profile(count, total, bound, slope), jnp.int32)
    couples = (count - 1) // 2
    donor, sink = lengths[1:1 + 2 * couples:2], lengths[2:2 + 2 * couples:2]
    margin = jnp.minimum(donor - 1, bound - sink)
    moved = jax.random.randint(jax.random.fold_in(stream_key, 1), (couples,), 0, 1 << 20) % (margin + 1)
    lengths = lengths.at[1:1 + 2 * couples:2].set(donor - moved).at[2:2 + 2 * couples:2].set(sink + moved)
    return lengths[jax.random.permutation(jax.random.fold_in(stream_key, 2), count)]


def noise(own_key, extent, scale, bound, shards=(), kind=jnp.bfloat16):
    drawn = jax.random.normal(own_key, extent, jnp.float32) * scale
    if len(shards) > 0:
        drawn = shard_levels(own_key, extent, shards, -0.22, 0.18) * drawn
    return jnp.clip(drawn, min=-bound, max=bound).astype(kind)


def setup_inputs(seed: int = 0) -> dict:
    keys = jax.random.split(jax.random.key(seed), 20)
    token_ids = place_ends(ranked_ids(keys[0], (BATCH, LEN), VOCAB, 2), jax.random.fold_in(keys[0], 3), 0, VOCAB - 1).astype(jnp.int32)
    target_ids = place_ends(ranked_ids(keys[1], (BATCH, LEN), VOCAB, 2), jax.random.fold_in(keys[1], 3), 0, VOCAB - 1).astype(jnp.int32)
    segment_ids = jax.vmap(lambda own: jnp.searchsorted(jnp.cumsum(ragged(own, 4, LEN, LEN // 2, 2)), jnp.arange(LEN), side="right"))(jax.random.split(keys[2], BATCH)).reshape((BATCH, LEN)).astype(jnp.int32)
    token_embed = noise(keys[3], (VOCAB, D), 0.07, 0.41992188, ((0, 16),))
    pos_embed = noise(keys[4], (POS, D), 0.1, 0.59765625)
    final_gain = jnp.clip(1.0 + 0.1 * jax.random.normal(keys[5], (D,), jnp.float32), 0.5, 1.5).astype(jnp.bfloat16)
    final_bias = noise(keys[6], (D,), 0.2, 1.0)
    ln1_gain = jnp.clip(1.0 + 0.1 * jax.random.normal(keys[7], (N_SECTION, D), jnp.float32), 0.5, 1.5).astype(jnp.bfloat16)
    ln1_bias = noise(keys[8], (N_SECTION, D), 0.2, 1.0, ((0, 2),))
    qkv_weight = noise(keys[9], (N_SECTION, D, 3 * D), D ** -0.5, 0.21875, ((0, 2),))
    qv_bias = noise(keys[10], (N_SECTION, 2 * D), 0.2, 1.0, ((0, 2),))
    out_weight = noise(keys[11], (N_SECTION, D, D), (D // 8) ** -0.5, 0.625, ((0, 2),))
    out_bias = noise(keys[12], (N_SECTION, D), 0.2, 1.0, ((0, 2),))
    ln2_gain = jnp.clip(1.0 + 0.1 * jax.random.normal(keys[13], (N_SECTION, D), jnp.float32), 0.5, 1.5).astype(jnp.bfloat16)
    ln2_bias = noise(keys[14], (N_SECTION, D), 0.2, 1.0, ((0, 2),))
    fc_weight = noise(keys[15], (N_SECTION, D, FF), D ** -0.5, 0.21875, ((0, 2),))
    fc_bias = noise(keys[16], (N_SECTION, FF), 0.2, 1.0, ((0, 2),))
    proj_weight = noise(keys[17], (N_SECTION, FF, D), FF ** -0.5, 0.109375, ((0, 2),))
    proj_bias = noise(keys[18], (N_SECTION, D), 0.2, 1.0, ((0, 2),))
    return {"token_ids": token_ids, "target_ids": target_ids, "segment_ids": segment_ids, "token_embed": token_embed, "pos_embed": pos_embed, "final_gain": final_gain, "final_bias": final_bias, "ln1_gain": ln1_gain, "ln1_bias": ln1_bias, "qkv_weight": qkv_weight, "qv_bias": qv_bias, "out_weight": out_weight, "out_bias": out_bias, "ln2_gain": ln2_gain, "ln2_bias": ln2_bias, "fc_weight": fc_weight, "fc_bias": fc_bias, "proj_weight": proj_weight, "proj_bias": proj_bias}


HIGH = lax.Precision.HIGHEST

@jax.custom_vjp
def low(v):
    return lax.optimization_barrier(v.astype(jnp.bfloat16)).astype(jnp.float32)

@jax.custom_vjp
def low_back(v):
    return v

def low_keep(v):
    return (low(v), None)

def low_pass(kept, grad):
    return (grad,)

def back_keep(v):
    return (v, None)

def back_low(kept, grad):
    return (low(grad),)
low.defvjp(low_keep, low_pass)
low_back.defvjp(back_keep, back_low)

def product(left, right):
    return jnp.dot(left, right, precision=HIGH, preferred_element_type=jnp.float32)

def layer_norm(values, gain, offset):
    centre = lax.optimization_barrier(jnp.mean(values, axis=-1, keepdims=True))
    shifted = values - centre
    spread = lax.optimization_barrier(jnp.mean(shifted * shifted, axis=-1, keepdims=True))
    return shifted * lax.rsqrt(spread + 1e-05) * gain + offset

def positions(segment):
    places = jnp.arange(segment.shape[0], dtype=jnp.int32)
    change = jnp.concatenate([jnp.ones((1,), dtype=jnp.bool_), segment[1:] != segment[:-1]])
    starts = lax.cummax(jnp.where(change, places, jnp.zeros_like(places)), axis=0)
    return places - starts

def allowed_pairs(segment):
    places = jnp.arange(segment.shape[0], dtype=jnp.int32)
    return (places[:, None] >= places[None, :]) & (segment[:, None] == segment[None, :])

def block(hidden, weights, allowed):
    gain_one, offset_one, qkv_w, qv_b, out_w, out_b, gain_two, offset_two, fc_w, fc_b, proj_w, proj_b = weights
    length, width = hidden.shape
    normed = low(layer_norm(hidden, gain_one, offset_one))
    qkv_bias = jnp.concatenate([qv_b[:width], jnp.zeros((width,), jnp.float32), qv_b[width:]])
    joined = low(low_back(product(normed, low(qkv_w)) + qkv_bias))
    heads = joined.reshape(length, 3, HEADS, HD).transpose(1, 2, 0, 3)
    scores = low_back(jnp.einsum('hqd,hkd->hqk', heads[0], heads[1], precision=HIGH)) * HD ** (-0.5)
    scores = jnp.where(allowed[None], scores, -1e+30)
    peak = lax.optimization_barrier(jnp.max(scores, axis=-1, keepdims=True))
    raised = jnp.exp(scores - peak)
    probs = raised / lax.optimization_barrier(jnp.sum(raised, axis=-1, keepdims=True))
    mixed = jnp.einsum('hqk,hkd->hqd', low(probs), heads[2], precision=HIGH)
    attended = low(low_back(mixed.transpose(1, 0, 2).reshape(length, width)))
    after = hidden + low_back(product(attended, low(out_w))) + out_b
    normed_two = low(layer_norm(after, gain_two, offset_two))
    inner = low_back(product(normed_two, low(fc_w)) + fc_b)
    active = low(jax.nn.gelu(inner, approximate=True))
    return after + low_back(product(active, low(proj_w))) + proj_b

def sequence_loss(params, row_ids, row_targets, segment):
    table, pos_table, fin_gain, fin_bias, layers = params
    places = positions(segment)
    hidden = table[row_ids] + pos_table[places]
    allowed = allowed_pairs(segment)
    for index in range(N_SECTION):
        hidden = block(hidden, tuple((weight[index] for weight in layers)), allowed)
    normed = low(layer_norm(hidden, fin_gain, fin_bias))
    logits = low_back(product(normed, low(table).T))
    top = jax.nn.logsumexp(logits, axis=-1)
    picked = jnp.take_along_axis(logits, row_targets[:, None], axis=-1)[:, 0]
    return jnp.mean(top - picked)

def reference(token_ids, target_ids, segment_ids, token_embed, pos_embed, final_gain, final_bias, ln1_gain, ln1_bias, qkv_weight, qv_bias, out_weight, out_bias, ln2_gain, ln2_bias, fc_weight, fc_bias, proj_weight, proj_bias):
    layers = tuple((weight.astype(jnp.float32) for weight in (ln1_gain, ln1_bias, qkv_weight, qv_bias, out_weight, out_bias, ln2_gain, ln2_bias, fc_weight, fc_bias, proj_weight, proj_bias)))
    params = (token_embed.astype(jnp.float32), pos_embed.astype(jnp.float32), final_gain.astype(jnp.float32), final_bias.astype(jnp.float32), layers)
    stepped = jax.checkpoint(sequence_loss)

    def objective(params_now):

        def accumulate(total, row):
            return (total + stepped(params_now, row[0], row[1], row[2]), None)
        total, _ = lax.scan(accumulate, jnp.zeros((), jnp.float32), (token_ids, target_ids, segment_ids))
        return total
    total, pull = jax.vjp(objective, params)
    grads = pull(jnp.ones((), jnp.float32))[0]
    layer_grads = grads[4]
    return (total / token_ids.shape[0], grads[0], grads[1], grads[2], grads[3], layer_grads[0], layer_grads[1], layer_grads[2], layer_grads[3], layer_grads[4], layer_grads[5], layer_grads[6], layer_grads[7], layer_grads[8], layer_grads[9], layer_grads[10], layer_grads[11])
```

```python
import math

import jax
import jax.numpy as jnp
from jax import lax
from jax.experimental import pallas as pl
from jax.experimental.pallas import tpu as pltpu
from jax.sharding import PartitionSpec as P

HEADS = 12
HD = 64
BF = jnp.bfloat16
F32 = jnp.float32
META = 128
VMEM_LIMIT = 60 * 1024 * 1024


def nn(left, right):
    return lax.dot_general(left, right, (((1,), (0,)), ((), ())), preferred_element_type=F32)


def nt(left, right):
    return lax.dot_general(left, right, (((1,), (1,)), ((), ())), preferred_element_type=F32)


def tn(left, right):
    return lax.dot_general(left, right, (((0,), (0,)), ((), ())), preferred_element_type=F32)


def normalised(values):
    centre = jnp.mean(values, axis=-1, keepdims=True)
    shifted = values - centre
    spread = jnp.mean(shifted * shifted, axis=-1, keepdims=True)
    scale = lax.rsqrt(spread + 1e-05)
    return shifted * scale, scale


def norm_back(grad, gain, hat, scale):
    ghat = grad * gain
    first = jnp.mean(ghat, axis=-1, keepdims=True)
    second = jnp.mean(ghat * hat, axis=-1, keepdims=True)
    return scale * (ghat - first - hat * second)


def rowsum(values):
    return jnp.sum(values, axis=0, keepdims=True)


TANH_SCALE = math.sqrt(2.0 / math.pi)


def gelu_parts(inner):
    square = inner * inner
    bend = jnp.tanh(TANH_SCALE * (inner + 0.044715 * (square * inner)))
    return 0.5 * (1.0 + bend), bend, square


def pair_masks(length):
    lane = lax.broadcasted_iota(jnp.int32, (length, 2 * HD), 1)
    return lane < HD


def stacked(values, even):
    zero = jnp.zeros_like(values)
    return jnp.concatenate(
        [jnp.where(even, values, zero), jnp.where(even, zero, values)], axis=0
    )


def pair_probs(queries, key_stack, allowed, length):
    scores = nt(queries, key_stack) * HD ** (-0.5)
    probs = []
    for part in range(2):
        own = jnp.where(allowed, scores[:, part * length : (part + 1) * length], -1e30)
        peak = jnp.max(own, axis=-1, keepdims=True)
        raised = jnp.exp(own - peak)
        probs.append(raised * (1.0 / jnp.sum(raised, axis=-1, keepdims=True)))
    return probs


def allowed_of(segc_ref, segr_ref, seq, length):
    rows = lax.broadcasted_iota(jnp.int32, (length, length), 0)
    cols = lax.broadcasted_iota(jnp.int32, (length, length), 1)
    same = segc_ref[pl.ds(seq * length, length), :] == segr_ref[pl.ds(seq, 1), :]
    return (rows >= cols) & same


def start_copies(pairs, sems):
    copies = [pltpu.make_async_copy(src, dst, sems.at[i]) for i, (src, dst) in enumerate(pairs)]
    for copy in copies:
        copy.start()
    return copies


def forward_kernel(
    x_ref, segc_ref, segr_ref, g1, b1, bqkv, bo, g2, b2, bfc, bproj,
    wqkv_h, wo_h, wfc_h, wproj_h, *rest, save,
):
    if save:
        y_ref, a1_ref, qkv_ref, att_ref, x1_ref, a2_ref, inner_ref, act_ref = rest[:8]
        wqkv, wo, wfc, wproj, sems = rest[8:]
    else:
        y_ref, qkv_ref, att_ref, wqkv, wo, wfc, wproj, sems = rest
    copies = start_copies(
        ((wqkv_h.at[0], wqkv), (wo_h.at[0], wo), (wfc_h.at[0], wfc), (wproj_h.at[0], wproj)), sems
    )
    micro, length = segr_ref.shape
    width = x_ref.shape[1]
    hidden = x_ref[...]
    hat, _ = normalised(hidden)
    a1 = (hat * g1[...] + b1[...]).astype(BF)
    if save:
        a1_ref[...] = a1
    copies[0].wait()
    for part in range(3):
        cols = slice(part * width, (part + 1) * width)
        qkv_ref[:, cols] = (nn(a1, wqkv[:, cols]) + bqkv[:, cols]).astype(BF)
    even = pair_masks(length)
    for seq in range(micro):
        allowed = allowed_of(segc_ref, segr_ref, seq, length)
        rows = slice(seq * length, (seq + 1) * length)
        for pair in range(HEADS // 2):
            lo = pair * 2 * HD
            queries = qkv_ref[rows, lo : lo + 2 * HD]
            key_stack = stacked(qkv_ref[rows, width + lo : width + lo + 2 * HD], even)
            value_stack = stacked(qkv_ref[rows, 2 * width + lo : 2 * width + lo + 2 * HD], even)
            probs = pair_probs(queries, key_stack, allowed, length)
            joined = jnp.concatenate([part.astype(BF) for part in probs], axis=1)
            att_ref[rows, lo : lo + 2 * HD] = nn(joined, value_stack).astype(BF)
    copies[1].wait()
    x1 = hidden + nn(att_ref[...], wo[...]) + bo[...]
    hat2, _ = normalised(x1)
    a2 = (hat2 * g2[...] + b2[...]).astype(BF)
    if save:
        x1_ref[...] = x1
        a2_ref[...] = a2
    copies[2].wait()
    copies[3].wait()
    total = x1 + bproj[...]
    hidden_units = wfc.shape[1]
    for part in range(hidden_units // width):
        cols = slice(part * width, (part + 1) * width)
        inner = nn(a2, wfc[:, cols]) + bfc[:, cols]
        half, _, _ = gelu_parts(inner)
        act = (inner * half).astype(BF)
        if save:
            inner_ref[:, cols] = inner
            act_ref[:, cols] = act
        total = total + nn(act, wproj[cols, :])
    y_ref[...] = total


def any_spec():
    return pl.BlockSpec(memory_space=pl.ANY)


def vmem_spec():
    return pl.BlockSpec(memory_space=pltpu.VMEM)


def params():
    return pltpu.CompilerParams(vmem_limit_bytes=VMEM_LIMIT)


def forward_layer(hidden, seg_col, seg_row, vectors, weights, save):
    rows, width = hidden.shape
    units = weights[2].shape[2]
    wide = weights[0].shape[2]
    sds = jax.ShapeDtypeStruct
    outs = [sds((rows, width), F32)]
    scratch = []
    if save:
        outs += [
            sds((rows, width), BF), sds((rows, wide), BF), sds((rows, width), BF),
            sds((rows, width), F32), sds((rows, width), BF), sds((rows, units), F32),
            sds((rows, units), BF),
        ]
    else:
        scratch = [pltpu.VMEM((rows, wide), BF), pltpu.VMEM((rows, width), BF)]
    scratch = scratch + [pltpu.VMEM(w.shape[1:], BF) for w in weights]
    scratch.append(pltpu.SemaphoreType.DMA((4,)))

    def kernel(*refs):
        forward_kernel(*refs, save=save)

    return pl.pallas_call(
        kernel,
        out_shape=outs,
        in_specs=[vmem_spec()] * 11 + [any_spec()] * 4,
        out_specs=[vmem_spec()] * len(outs),
        scratch_shapes=scratch,
        compiler_params=params(),
        name="layer_forward_save" if save else "layer_forward",
    )(hidden, seg_col, seg_row, *vectors, *weights)


def mlp_back_kernel(dy_ref, x1_ref, inner_ref, g2, wfc_h, wproj_h, *rest, save):
    if save:
        dx1_ref, gy_ref, gin_ref, dg2, db2, dfc, dproj, wfc, wproj, sems = rest
    else:
        dx1_ref, wfc, wproj, sems = rest
    copies = start_copies(((wproj_h.at[0], wproj), (wfc_h.at[0], wfc)), sems)
    width = dy_ref.shape[1]
    units = inner_ref.shape[1]
    dy = dy_ref[...]
    gy = dy.astype(BF)
    if save:
        gy_ref[...] = gy
        dproj[...] = rowsum(dy)
    hat, scale = normalised(x1_ref[...])
    copies[0].wait()
    copies[1].wait()
    da2 = jnp.zeros(dy.shape, F32)
    for part in range(units // width):
        cols = slice(part * width, (part + 1) * width)
        dact = nt(gy, wproj[cols, :])
        inner = inner_ref[:, cols]
        half, bend, square = gelu_parts(inner)
        slope = half + (0.5 * TANH_SCALE) * inner * (1.0 - bend * bend) * (
            1.0 + (3 * 0.044715) * square
        )
        gin = (dact * slope).astype(BF)
        if save:
            gin_ref[:, cols] = gin
            dfc[:, cols] = rowsum(gin.astype(F32))
        da2 = da2 + nt(gin, wfc[:, cols])
    if save:
        dg2[...] = rowsum(da2 * hat)
        db2[...] = rowsum(da2)
    dx1_ref[...] = dy + norm_back(da2, g2[...], hat, scale)


def mlp_back(dy, x1, inner, gain, wfc, wproj, save):
    rows, width = dy.shape
    units = inner.shape[1]
    sds = jax.ShapeDtypeStruct
    outs = [sds((rows, width), F32)]
    if save:
        outs += [
            sds((rows, width), BF), sds((rows, units), BF), sds((1, width), F32),
            sds((1, width), F32), sds((1, units), F32), sds((1, width), F32),
        ]

    def kernel(*refs):
        mlp_back_kernel(*refs, save=save)

    return pl.pallas_call(
        kernel,
        out_shape=outs,
        in_specs=[vmem_spec()] * 4 + [any_spec()] * 2,
        out_specs=[vmem_spec()] * len(outs),
        scratch_shapes=[
            pltpu.VMEM(wfc.shape[1:], BF), pltpu.VMEM(wproj.shape[1:], BF),
            pltpu.SemaphoreType.DMA((2,)),
        ],
        compiler_params=params(),
        name="mlp_back_save" if save else "mlp_back",
    )(dy, x1, inner, gain, wfc, wproj)


def att_back_kernel(dx1_ref, x_ref, qkv_ref, segc_ref, segr_ref, g1, wqkv_h, wo_h, *rest, save):
    if save:
        dx_ref, gx1_ref, dqkv_ref, dg1, db1, dbqkv, dbo, datt_ref, wqkv, wo, sems = rest
    else:
        dx_ref, dqkv_ref, datt_ref, wqkv, wo, sems = rest
    copies = start_copies(((wo_h.at[0], wo), (wqkv_h.at[0], wqkv)), sems)
    micro, length = segr_ref.shape
    width = x_ref.shape[1]
    dx1 = dx1_ref[...]
    gx1 = dx1.astype(BF)
    if save:
        gx1_ref[...] = gx1
        dbo[...] = rowsum(dx1)
    copies[0].wait()
    datt_ref[...] = nt(gx1, wo[...]).astype(BF)
    even = pair_masks(length)
    for seq in range(micro):
        allowed = allowed_of(segc_ref, segr_ref, seq, length)
        rows = slice(seq * length, (seq + 1) * length)
        for pair in range(HEADS // 2):
            lo = pair * 2 * HD
            queries = qkv_ref[rows, lo : lo + 2 * HD]
            key_stack = stacked(qkv_ref[rows, width + lo : width + lo + 2 * HD], even)
            value_stack = stacked(qkv_ref[rows, 2 * width + lo : 2 * width + lo + 2 * HD], even)
            probs = pair_probs(queries, key_stack, allowed, length)
            dmix = datt_ref[rows, lo : lo + 2 * HD]
            dprobs = nt(dmix, value_stack)
            low = []
            dscores = []
            for part in range(2):
                dp = dprobs[:, part * length : (part + 1) * length]
                inside = jnp.sum(probs[part] * dp, axis=-1, keepdims=True)
                ds = probs[part] * (dp - inside)
                dscores.append((ds * HD ** (-0.5)).astype(BF))
                low.append(probs[part].astype(BF))
            dq = nn(jnp.concatenate(dscores, axis=1), key_stack)
            dk = tn(jnp.concatenate(dscores, axis=0), stacked(queries, even))
            dv = tn(jnp.concatenate(low, axis=0), stacked(dmix, even))
            dqkv_ref[rows, lo : lo + 2 * HD] = dq.astype(BF)
            dqkv_ref[rows, width + lo : width + lo + 2 * HD] = dk.astype(BF)
            dqkv_ref[rows, 2 * width + lo : 2 * width + lo + 2 * HD] = dv.astype(BF)
    hat, scale = normalised(x_ref[...])
    copies[1].wait()
    da1 = jnp.zeros(dx1.shape, F32)
    for part in range(3):
        cols = slice(part * width, (part + 1) * width)
        piece = dqkv_ref[:, cols]
        if save:
            dbqkv[:, cols] = rowsum(piece.astype(F32))
        da1 = da1 + nt(piece, wqkv[:, cols])
    if save:
        dg1[...] = rowsum(da1 * hat)
        db1[...] = rowsum(da1)
    dx_ref[...] = dx1 + norm_back(da1, g1[...], hat, scale)


def att_back(dx1, hidden, qkv, seg_col, seg_row, gain, wqkv, wo, save):
    rows, width = dx1.shape
    wide = qkv.shape[1]
    sds = jax.ShapeDtypeStruct
    outs = [sds((rows, width), F32)]
    scratch = []
    if save:
        outs += [
            sds((rows, width), BF), sds((rows, wide), BF), sds((1, width), F32),
            sds((1, width), F32), sds((1, wide), F32), sds((1, width), F32),
        ]
    else:
        scratch = [pltpu.VMEM((rows, wide), BF)]
    scratch = scratch + [
        pltpu.VMEM((rows, width), BF), pltpu.VMEM(wqkv.shape[1:], BF),
        pltpu.VMEM(wo.shape[1:], BF), pltpu.SemaphoreType.DMA((2,)),
    ]

    def kernel(*refs):
        att_back_kernel(*refs, save=save)

    return pl.pallas_call(
        kernel,
        out_shape=outs,
        in_specs=[vmem_spec()] * 6 + [any_spec()] * 2,
        out_specs=[vmem_spec()] * len(outs),
        scratch_shapes=scratch,
        compiler_params=params(),
        name="att_back_save" if save else "att_back",
    )(dx1, hidden, qkv, seg_col, seg_row, gain, wqkv, wo)


def head_kernel(
    h_ref, tgt_ref, gain, offset, table_ref,
    dh_ref, ext_ref, dgain, doff, loss_ref,
    logits, top, total, picked, dhn, length,
):
    turn = pl.program_id(0)
    block = pl.program_id(1)
    blocks = pl.num_programs(1)
    rows, width = h_ref.shape
    size = table_ref.shape[0]

    @pl.when((turn == 0) & (block == 0))
    def _():
        hat, _ = normalised(h_ref[...])
        ext_ref[:, :width] = (hat * gain[...] + offset[...]).astype(BF)
        top[...] = jnp.full(top.shape, -1e30, F32)
        total[...] = jnp.zeros(total.shape, F32)
        picked[...] = jnp.zeros(picked.shape, F32)
        dhn[...] = jnp.zeros(dhn.shape, F32)

    words = block * size + lax.broadcasted_iota(jnp.int32, (rows, size), 1)
    hits = words == tgt_ref[...]

    @pl.when(turn == 0)
    def _():
        piece = nt(ext_ref[:, :width], table_ref[...])
        logits[block] = piece
        now = jnp.maximum(top[...], jnp.max(piece, axis=1, keepdims=True))
        total[...] = total[...] * jnp.exp(top[...] - now) + jnp.sum(
            jnp.exp(piece - now), axis=1, keepdims=True
        )
        top[...] = now
        picked[...] += jnp.sum(jnp.where(hits, piece, 0.0), axis=1, keepdims=True)

    @pl.when((turn == 1) & (block == 0))
    def _():
        top[...] = top[...] + jnp.log(total[...])
        lse = top[...]
        loss_ref[...] = jnp.sum(lse - picked[...], axis=0, keepdims=True) / length
        high = lse.astype(BF).astype(F32)
        mid = (lse - high).astype(BF).astype(F32)
        low = lse - high - mid
        tgt = tgt_ref[...]
        tgt_high = (tgt >> 8).astype(F32)
        tgt_low = (tgt & 255).astype(F32)
        lane = lax.broadcasted_iota(jnp.int32, (rows, META), 1)
        meta = jnp.zeros((rows, META), F32)
        for index, column in enumerate((high, mid, low, tgt_high, tgt_low)):
            meta = jnp.where(lane == index, column, meta)
        ext_ref[:, width:] = meta.astype(BF)

    @pl.when(turn == 1)
    def _():
        probs = jnp.exp(logits[block] - top[...])
        dlog = ((probs - hits.astype(F32)) / length).astype(BF)
        dhn[...] += nn(dlog, table_ref[...])

    @pl.when((turn == 1) & (block == blocks - 1))
    def _():
        hat, scale = normalised(h_ref[...])
        grad = dhn[...]
        dgain[...] = rowsum(grad * hat)
        doff[...] = rowsum(grad)
        dh_ref[...] = norm_back(grad, gain[...], hat, scale)


def head(hidden, targets, gain, offset, table, length):
    rows, width = hidden.shape
    vocab = table.shape[0]
    size = math.gcd(vocab, 1024)
    blocks = vocab // size
    sds = jax.ShapeDtypeStruct

    def kernel(*refs):
        head_kernel(*refs, length=length)

    def full(shape):
        return pl.BlockSpec(shape, lambda t, b: (0,) * len(shape))

    outs = [
        sds((rows, width), F32), sds((rows, width + META), BF), sds((1, width), F32),
        sds((1, width), F32), sds((1, 1), F32),
    ]
    return pl.pallas_call(
        kernel,
        grid=(2, blocks),
        out_shape=outs,
        in_specs=[
            full((rows, width)), full((rows, 1)), full((1, width)), full((1, width)),
            pl.BlockSpec((size, width), lambda t, b: (b, 0)),
        ],
        out_specs=[full(out.shape) for out in outs],
        scratch_shapes=[
            pltpu.VMEM((blocks, rows, size), F32), pltpu.VMEM((rows, 1), F32),
            pltpu.VMEM((rows, 1), F32), pltpu.VMEM((rows, 1), F32),
            pltpu.VMEM((rows, width), F32),
        ],
        compiler_params=params(),
        name="head",
    )(hidden, targets, gain, offset, table)


def table_kernel(base_ref, ext_ref, shard_ref, out_ref, *, length):
    width = shard_ref.shape[1]
    size = shard_ref.shape[0]
    rows = ext_ref.shape[0]

    @pl.when(pl.program_id(0) == 0)
    def _():
        out_ref[...] = jnp.zeros(out_ref.shape, F32)

    hn = ext_ref[:, :width]
    meta = ext_ref[:, width:].astype(F32)
    lse = meta[:, 0:1] + meta[:, 1:2] + meta[:, 2:3]
    target = meta[:, 3:4] * 256.0 + meta[:, 4:5]
    words = (base_ref[0] + lax.broadcasted_iota(jnp.int32, (rows, size), 1)).astype(F32)
    probs = jnp.exp(nt(hn, shard_ref[...]) - lse)
    dlog = ((probs - (words == target).astype(F32)) / length).astype(BF)
    out_ref[...] += tn(dlog, hn)


def table_head(base, ext, shard, length):
    rows = ext.shape[0]
    step = math.gcd(rows, 512)
    width = shard.shape[1]

    def kernel(*refs):
        table_kernel(*refs, length=length)

    return pl.pallas_call(
        kernel,
        grid=(rows // step,),
        out_shape=jax.ShapeDtypeStruct(shard.shape, F32),
        in_specs=[
            pl.BlockSpec(memory_space=pltpu.SMEM),
            pl.BlockSpec((step, width + META), lambda r: (r, 0)),
            pl.BlockSpec(shard.shape, lambda r: (0, 0)),
        ],
        out_specs=pl.BlockSpec(shard.shape, lambda r: (0, 0)),
        compiler_params=params(),
        name="table_head",
    )(base, ext, shard)


def lookup_kernel(base_ref, ext_ref, table_out, pos_out):
    width = table_out.shape[1]
    rows = ext_ref.shape[0]

    @pl.when(pl.program_id(0) == 0)
    def _():
        table_out[...] = jnp.zeros(table_out.shape, F32)
        pos_out[...] = jnp.zeros(pos_out.shape, F32)

    dx = ext_ref[:, :width]
    meta = ext_ref[:, width:].astype(F32)
    token = meta[:, 0:1] * 256.0 + meta[:, 1:2]
    place = meta[:, 2:3] * 256.0 + meta[:, 3:4]
    for index, (value, out) in enumerate(((token, table_out), (place, pos_out))):
        size = out.shape[0]
        names = (base_ref[index] + lax.broadcasted_iota(jnp.int32, (rows, size), 1)).astype(F32)
        chosen = (names == value).astype(F32).astype(BF)
        out[...] += tn(chosen, dx)


def lookup_back(bases, ext, table_rows, pos_rows, width):
    rows = ext.shape[0]
    step = math.gcd(rows, 512)
    outs = [
        jax.ShapeDtypeStruct((table_rows, width), F32),
        jax.ShapeDtypeStruct((pos_rows, width), F32),
    ]
    return pl.pallas_call(
        lookup_kernel,
        grid=(rows // step,),
        out_shape=outs,
        in_specs=[
            pl.BlockSpec(memory_space=pltpu.SMEM),
            pl.BlockSpec((step, width + META), lambda r: (r, 0)),
        ],
        out_specs=[pl.BlockSpec(out.shape, lambda r: (0, 0)) for out in outs],
        compiler_params=params(),
        name="lookup_back",
    )(bases, ext)


class Line:
    def __init__(self):
        self.size = lax.axis_size("dp")
        self.line = self.size // 4
        self.index = lax.axis_index("dp")
        self.core = self.index % 2
        self.pair = (self.index // 2) % 2
        self.place = self.index // 4

    def swap(self, array, bit):
        return lax.ppermute(array, "dp", [(i, i ^ bit) for i in range(self.size)])

    def shift(self, array, by):
        step = 4 * by
        pairs = [(i, i + step) for i in range(self.size) if 0 <= i + step < self.size]
        return lax.ppermute(array, "dp", pairs)

    def pick(self, array, index):
        return lax.dynamic_index_in_dim(array, index % array.shape[0], 0, keepdims=False)

    def line_sum(self, parts):
        if self.line > 4:
            groups = [[4 * k + j for k in range(self.line)] for j in range(4)]
            return lax.psum_scatter(parts, "dp", scatter_dimension=0, axis_index_groups=groups)
        up = down = None
        for step in range(1, self.line):
            reach = self.line - step
            send_up = self.pick(parts, self.place + reach)
            send_down = self.pick(parts, self.place - reach + self.line)
            if up is not None:
                send_up = send_up + up.astype(F32)
                send_down = send_down + down.astype(F32)
            up = self.shift(send_up.astype(BF), 1)
            down = self.shift(send_down.astype(BF), -1)
        return self.pick(parts, self.place) + up.astype(F32) + down.astype(F32)

    def rows_for(self, transposed, pair, core):
        rows, tokens = transposed.shape
        split = transposed.reshape(self.line, 4, rows // self.size, tokens)
        chosen = lax.dynamic_index_in_dim(split, pair * 2 + core, 1, keepdims=False)
        return chosen.reshape(rows // 4, tokens)

    def weight_sum(self, activ, grads):
        keep, send = activ
        sent = self.swap(nn(send, grads).astype(BF), 2)
        own = nn(keep, grads) + sent.astype(F32)
        return self.line_sum(own.reshape(self.line, -1, own.shape[1]))

    def share(self, saved):
        flat = saved.T
        mine = [self.rows_for(flat, pair, self.core) for pair in (self.pair, 1 - self.pair)]
        theirs = [self.rows_for(flat, pair, 1 - self.core) for pair in (self.pair, 1 - self.pair)]
        got = self.swap(jnp.concatenate(theirs, axis=0), 1)
        half = got.shape[0] // 2
        return (
            jnp.concatenate([mine[0], got[:half]], axis=1),
            jnp.concatenate([mine[1], got[half:]], axis=1),
        )

    def both(self, grads):
        return jnp.concatenate([grads, self.swap(grads, 1)], axis=0)


def body(
    token_ids, target_ids, segment_ids, token_embed, pos_embed, final_gain, final_bias,
    ln1_gain, ln1_bias, qkv_weight, qv_bias, out_weight, out_bias, ln2_gain, ln2_bias,
    fc_weight, fc_bias, proj_weight, proj_bias,
):
    on_first = lax.axis_index("section") == 0
    line = Line()
    micro, length = token_ids.shape
    rows = micro * length
    shard, width = token_embed.shape
    pos_shard = pos_embed.shape[0] // line.size

    full_table = lax.all_gather(token_embed, "dp", axis=0, tiled=True)
    earlier = segment_ids[:, None, :] < segment_ids[:, :, None]
    places = jnp.arange(length, dtype=jnp.int32)[None, :] - jnp.sum(
        earlier.astype(jnp.int32), axis=2
    )
    flat_places = places.reshape(-1)
    flat_ids = token_ids.reshape(-1)
    embedded = jnp.take(full_table, flat_ids, axis=0).astype(F32) + jnp.take(
        pos_embed, flat_places, axis=0
    ).astype(F32)

    seg_col = segment_ids.reshape(rows, 1)
    bqkv = jnp.concatenate(
        [qv_bias[:, :width], jnp.zeros((1, width), qv_bias.dtype), qv_bias[:, width:]], axis=1
    )
    vectors = [
        v.astype(F32)
        for v in (ln1_gain, ln1_bias, bqkv, out_bias, ln2_gain, ln2_bias, fc_bias, proj_bias)
    ]
    weights = (qkv_weight, out_weight, fc_weight, proj_weight)

    (first_out,) = forward_layer(embedded, seg_col, segment_ids, vectors, weights, False)
    incoming = lax.ppermute(first_out, "section", [(0, 1)])
    hidden = jnp.where(on_first, embedded, incoming)
    out, a1, qkv, att, x1, a2, inner, act = forward_layer(
        hidden, seg_col, segment_ids, vectors, weights, True
    )
    gain = final_gain.astype(F32)[None]
    offset = final_bias.astype(F32)[None]
    dh, ext, dgain, doff, loss = head(
        out, target_ids.reshape(rows, 1), gain, offset, full_table, length
    )
    half = rows // 2
    ext_moved = lax.ppermute(ext[half:], "section", [(1, 0)])
    ext_own = jnp.where(on_first, ext_moved, ext[:half])
    ext_all = lax.all_gather(ext_own, "dp", axis=0, tiled=True)

    shared = [line.share(saved) for saved in (a1, att, a2, act)]

    (mid,) = mlp_back(dh, x1, inner, vectors[4], fc_weight, proj_weight, False)
    (back,) = att_back(mid, hidden, qkv, seg_col, segment_ids, vectors[0], qkv_weight, out_weight, False)
    upstream = jnp.where(on_first, lax.ppermute(back, "section", [(1, 0)]), dh)
    dx1, gy, gin, dg2, db2, dfc, dproj = mlp_back(
        upstream, x1, inner, vectors[4], fc_weight, proj_weight, True
    )
    proj_share = line.weight_sum(shared[3], line.both(gy))
    fc_share = line.weight_sum(shared[2], line.both(gin))
    dx0, gx1, dqkv, dg1, db1, dbqkv, dbo = att_back(
        dx1, hidden, qkv, seg_col, segment_ids, vectors[0], qkv_weight, out_weight, True
    )
    out_share = line.weight_sum(shared[1], line.both(gx1))
    qkv_share = line.weight_sum(shared[0], line.both(dqkv))

    base = line.index * shard
    table_part = table_head(base.reshape(1), ext_all, token_embed, length)

    lane = jnp.arange(META, dtype=jnp.int32)[None, :]
    meta = jnp.zeros((rows, META), F32)
    for index, column in enumerate(
        (flat_ids >> 8, flat_ids & 255, flat_places >> 8, flat_places & 255)
    ):
        meta = jnp.where(lane == index, column.astype(F32)[:, None], meta)
    dx_ext = jnp.concatenate([dx0.astype(BF), meta.astype(BF)], axis=1)
    dx_moved = lax.ppermute(dx_ext[half:], "section", [(0, 1)])
    dx_own = jnp.where(on_first, dx_ext[:half], dx_moved)
    dx_all = lax.all_gather(dx_own, "dp", axis=0, tiled=True)
    bases = jnp.stack([base, line.index * pos_shard])
    lookup, pos_part = lookup_back(bases, dx_all, shard, pos_shard, width)

    masked = [jnp.where(on_first, 0.0, v) for v in (dgain, doff)]
    small = [dg1, db1, dbqkv[:, :width], dbqkv[:, 2 * width :], dbo, dg2, db2, dfc, dproj]
    qv = jnp.concatenate(small[2:4], axis=1)
    small = [small[0], small[1], qv] + small[4:] + masked
    widths = [v.shape[1] // line.size for v in small]
    loss_own = jnp.where(on_first, 0.0, loss[0, 0])
    packed = jnp.concatenate(
        [v.reshape(line.size, -1) for v in small] + [jnp.full((line.size, 1), loss_own, F32)],
        axis=1,
    )
    summed = jnp.sum(lax.all_to_all(packed, "dp", 0, 0, tiled=True), axis=0)
    pieces = []
    at = 0
    for size in widths:
        pieces.append(summed[at : at + size])
        at += size
    tail = summed[sum(widths[:-2]) :]
    both = [(0, 1), (1, 0)]
    tail = tail + lax.ppermute(tail, "section", both)
    g_fin, b_fin = tail[: widths[-2]], tail[widths[-2] : widths[-2] + widths[-1]]
    loss_value = tail[-1] / (micro * line.size)
    table_sum = table_part + lax.ppermute(table_part, "section", both)
    late = jnp.concatenate([lookup, pos_part], axis=0)
    late = lax.reduce_precision(late, 8, 7)
    late = late + lax.ppermute(late.astype(BF), "section", both).astype(F32)
    table_sum = table_sum + late[:shard]
    pos_sum = late[shard:]
    return (
        loss_value, table_sum, pos_sum, g_fin, b_fin,
        pieces[0][None], pieces[1][None], qkv_share[None], pieces[2][None], out_share[None],
        pieces[3][None], pieces[4][None], pieces[5][None], fc_share[None], pieces[6][None],
        proj_share[None], pieces[7][None],
    )


def solution(mesh):
    in_specs = (
        P("dp", None), P("dp", None), P("dp", None), P("dp", None), P(), P(), P(),
        P("section", None), P("section", None), P("section", None, None), P("section", None),
        P("section", None, None), P("section", None), P("section", None), P("section", None),
        P("section", None, None), P("section", None), P("section", None, None), P("section", None),
    )
    out_specs = (
        P(), P("dp", None), P("dp", None), P("dp"), P("dp"),
        P("section", "dp"), P("section", "dp"), P("section", "dp", None), P("section", "dp"),
        P("section", "dp", None), P("section", "dp"), P("section", "dp"), P("section", "dp"),
        P("section", "dp", None), P("section", "dp"), P("section", "dp", None),
        P("section", "dp"),
    )
    return jax.shard_map(body, mesh=mesh, in_specs=in_specs, out_specs=out_specs, check_vma=False)
```

```python
import math

import jax
import jax.numpy as jnp
from jax import lax
from jax.experimental import pallas as pl
from jax.experimental.pallas import tpu as pltpu
from jax.sharding import PartitionSpec as P


HEADS = 12
HD = 64
BF = jnp.bfloat16
F32 = jnp.float32
META = 128
VMEM_LIMIT = 60 * 1024 * 1024


def nn(left, right):
    return lax.dot_general(left, right, (((1,), (0,)), ((), ())), preferred_element_type=F32)


def nt(left, right):
    return lax.dot_general(left, right, (((1,), (1,)), ((), ())), preferred_element_type=F32)


def tn(left, right):
    return lax.dot_general(left, right, (((0,), (0,)), ((), ())), preferred_element_type=F32)


def normalised(values):
    centre = jnp.mean(values, axis=-1, keepdims=True)
    shifted = values - centre
    spread = jnp.mean(shifted * shifted, axis=-1, keepdims=True)
    scale = lax.rsqrt(spread + 1e-05)
    return shifted * scale, scale


def norm_back(grad, gain, hat, scale):
    ghat = grad * gain
    first = jnp.mean(ghat, axis=-1, keepdims=True)
    second = jnp.mean(ghat * hat, axis=-1, keepdims=True)
    return scale * (ghat - first - hat * second)


def rowsum(values):
    return jnp.sum(values, axis=0, keepdims=True)


TANH_SCALE = math.sqrt(2.0 / math.pi)


def gelu_parts(inner):
    square = inner * inner
    bend = jnp.tanh(TANH_SCALE * (inner + 0.044715 * (square * inner)))
    return 0.5 * (1.0 + bend), bend, square


def pair_masks(length):
    lane = lax.broadcasted_iota(jnp.int32, (length, 2 * HD), 1)
    return lane < HD


def stacked(values, even):
    zero = jnp.zeros_like(values)
    return jnp.concatenate(
        [jnp.where(even, values, zero), jnp.where(even, zero, values)], axis=0
    )


def pair_probs(queries, key_stack, allowed, length):
    scores = nt(queries, key_stack) * HD ** (-0.5)
    probs = []
    for part in range(2):
        own = jnp.where(allowed, scores[:, part * length : (part + 1) * length], -1e30)
        peak = jnp.max(own, axis=-1, keepdims=True)
        raised = jnp.exp(own - peak)
        probs.append(raised * (1.0 / jnp.sum(raised, axis=-1, keepdims=True)))
    return probs


def allowed_of(segc_ref, segr_ref, seq, length):
    rows = lax.broadcasted_iota(jnp.int32, (length, length), 0)
    cols = lax.broadcasted_iota(jnp.int32, (length, length), 1)
    same = segc_ref[pl.ds(seq * length, length), :] == segr_ref[pl.ds(seq, 1), :]
    return (rows >= cols) & same


def start_copies(pairs, sems):
    copies = [pltpu.make_async_copy(src, dst, sems.at[i]) for i, (src, dst) in enumerate(pairs)]
    for copy in copies:
        copy.start()
    return copies


def forward_kernel(
    x_ref, segc_ref, segr_ref, g1, b1, bqkv, bo, g2, b2, bfc, bproj,
    wqkv_h, wo_h, wfc_h, wproj_h, *rest, save,
):
    width = x_ref.shape[1]
    if save:
        come_ref, first, y_ref, hid_ref, acts_ref, qkv_ref, x1_ref, inner_ref, act_ref = rest[:9]
        att_at = width
        wqkv, wo, wfc, wproj, sems = rest[9:]
    else:
        y_ref, qkv_ref, acts_ref, wqkv, wo, wfc, wproj, sems = rest
        att_at = 0
    copies = start_copies(
        ((wqkv_h.at[0], wqkv), (wo_h.at[0], wo), (wfc_h.at[0], wfc), (wproj_h.at[0], wproj)), sems
    )
    micro, length = segr_ref.shape
    hidden = x_ref[...]
    if save:
        hidden = jnp.where(first[0] == 1, hidden, come_ref[...].astype(F32))
        hid_ref[...] = hidden
    hat, _ = normalised(hidden)
    a1 = (hat * wide(g1) + wide(b1)).astype(BF)
    if save:
        acts_ref[:, :width] = a1
    copies[0].wait()
    for part in range(3):
        cols = slice(part * width, (part + 1) * width)
        qkv_ref[:, cols] = (nn(a1, wqkv[:, cols]) + bqkv[:, cols].astype(F32)).astype(BF)
    even = pair_masks(length)
    for seq in range(micro):
        allowed = allowed_of(segc_ref, segr_ref, seq, length)
        rows = slice(seq * length, (seq + 1) * length)
        for pair in range(HEADS // 2):
            lo = pair * 2 * HD
            queries = qkv_ref[rows, lo : lo + 2 * HD]
            key_stack = stacked(qkv_ref[rows, width + lo : width + lo + 2 * HD], even)
            value_stack = stacked(qkv_ref[rows, 2 * width + lo : 2 * width + lo + 2 * HD], even)
            probs = pair_probs(queries, key_stack, allowed, length)
            joined = jnp.concatenate([part.astype(BF) for part in probs], axis=1)
            acts_ref[rows, att_at + lo : att_at + lo + 2 * HD] = nn(joined, value_stack).astype(BF)
    copies[1].wait()
    x1 = hidden + nn(acts_ref[:, att_at : att_at + width], wo[...]) + wide(bo)
    hat2, _ = normalised(x1)
    a2 = (hat2 * wide(g2) + wide(b2)).astype(BF)
    if save:
        x1_ref[...] = x1
        acts_ref[:, 2 * width :] = a2
    copies[2].wait()
    copies[3].wait()
    total = x1 + wide(bproj)
    hidden_units = wfc.shape[1]
    for part in range(hidden_units // width):
        cols = slice(part * width, (part + 1) * width)
        inner = nn(a2, wfc[:, cols]) + bfc[:, cols].astype(F32)
        half, _, _ = gelu_parts(inner)
        act = (inner * half).astype(BF)
        if save:
            inner_ref[:, cols] = inner
            act_ref[:, cols] = act
        total = total + nn(act, wproj[cols, :])
    y_ref[...] = total.astype(y_ref.dtype)


def wide(ref):
    return ref[...].astype(F32)


def any_spec():
    return pl.BlockSpec(memory_space=pl.ANY)


def vmem_spec():
    return pl.BlockSpec(memory_space=pltpu.VMEM)


def smem_spec():
    return pl.BlockSpec(memory_space=pltpu.SMEM)


def params():
    return pltpu.CompilerParams(vmem_limit_bytes=VMEM_LIMIT)


def forward_layer(hidden, seg_col, seg_row, vectors, weights, incoming=None, first=None):
    save = incoming is not None
    rows, width = hidden.shape
    units = weights[2].shape[2]
    span = weights[0].shape[2]
    sds = jax.ShapeDtypeStruct
    if save:
        outs = [
            sds((rows, width), F32), sds((rows, width), F32), sds((rows, 3 * width), BF),
            sds((rows, span), BF), sds((rows, width), F32), sds((rows, units), F32),
            sds((rows, units), BF),
        ]
        scratch = []
        extra, extra_specs = (incoming, first), [vmem_spec(), smem_spec()]
    else:
        outs = [sds((rows, width), BF)]
        scratch = [pltpu.VMEM((rows, span), BF), pltpu.VMEM((rows, width), BF)]
        extra, extra_specs = (), []
    scratch = scratch + [pltpu.VMEM(w.shape[1:], BF) for w in weights]
    scratch.append(pltpu.SemaphoreType.DMA((4,)))

    def kernel(*refs):
        forward_kernel(*refs, save=save)

    return pl.pallas_call(
        kernel,
        out_shape=outs,
        in_specs=[vmem_spec()] * 11 + [any_spec()] * 4 + extra_specs,
        out_specs=[vmem_spec()] * len(outs),
        scratch_shapes=scratch,
        compiler_params=params(),
        name="layer_forward_save" if save else "layer_forward",
    )(hidden, seg_col, seg_row, *vectors, *weights, *extra)


def mlp_back_kernel(dy_ref, x1_ref, inner_ref, g2, wfc_h, wproj_h, *rest, save):
    if save:
        gy_ref, first, dx1_ref, gin_ref, dg2, db2, dfc, dproj, wfc, wproj, sems = rest
    else:
        dx1_ref, wfc, wproj, sems = rest
    copies = start_copies(((wproj_h.at[0], wproj), (wfc_h.at[0], wfc)), sems)
    width = dy_ref.shape[1]
    units = inner_ref.shape[1]
    dy = dy_ref[...]
    if save:
        gy = gy_ref[...]
        dy = jnp.where(first[0] == 1, gy.astype(F32), dy)
        dproj[...] = rowsum(dy)
    else:
        gy = dy.astype(BF)
    hat, scale = normalised(x1_ref[...])
    copies[0].wait()
    copies[1].wait()
    da2 = jnp.zeros(dy.shape, F32)
    for part in range(units // width):
        cols = slice(part * width, (part + 1) * width)
        dact = nt(gy, wproj[cols, :])
        inner = inner_ref[:, cols]
        half, bend, square = gelu_parts(inner)
        slope = half + (0.5 * TANH_SCALE) * inner * (1.0 - bend * bend) * (
            1.0 + (3 * 0.044715) * square
        )
        gin = (dact * slope).astype(BF)
        if save:
            gin_ref[:, cols] = gin
            dfc[:, cols] = rowsum(gin.astype(F32))
        da2 = da2 + nt(gin, wfc[:, cols])
    if save:
        dg2[...] = rowsum(da2 * hat)
        db2[...] = rowsum(da2)
    dx1_ref[...] = dy + norm_back(da2, wide(g2), hat, scale)


def mlp_back(dy, x1, inner, gain, wfc, wproj, gy=None, first=None):
    save = gy is not None
    rows, width = dy.shape
    units = inner.shape[1]
    sds = jax.ShapeDtypeStruct
    outs = [sds((rows, width), F32)]
    extra, extra_specs = (), []
    if save:
        outs += [
            sds((rows, units), BF), sds((1, width), F32), sds((1, width), F32),
            sds((1, units), F32), sds((1, width), F32),
        ]
        extra, extra_specs = (gy, first), [vmem_spec(), smem_spec()]

    def kernel(*refs):
        mlp_back_kernel(*refs, save=save)

    return pl.pallas_call(
        kernel,
        out_shape=outs,
        in_specs=[vmem_spec()] * 4 + [any_spec()] * 2 + extra_specs,
        out_specs=[vmem_spec()] * len(outs),
        scratch_shapes=[
            pltpu.VMEM(wfc.shape[1:], BF), pltpu.VMEM(wproj.shape[1:], BF),
            pltpu.SemaphoreType.DMA((2,)),
        ],
        compiler_params=params(),
        name="mlp_back_save" if save else "mlp_back",
    )(dy, x1, inner, gain, wfc, wproj, *extra)


def att_back_kernel(dx1_ref, x_ref, qkv_ref, segc_ref, segr_ref, g1, wqkv_h, wo_h, *rest, save):
    if save:
        meta_ref, dx_ref, grads_ref, dg1, db1, dbqkv, dbo, datt_ref, wqkv, wo, sems = rest
    else:
        dx_ref, grads_ref, datt_ref, wqkv, wo, sems = rest
    copies = start_copies(((wo_h.at[0], wo), (wqkv_h.at[0], wqkv)), sems)
    micro, length = segr_ref.shape
    width = x_ref.shape[1]
    dx1 = dx1_ref[...]
    gx1 = dx1.astype(BF)
    if save:
        grads_ref[:, 3 * width :] = gx1
        dbo[...] = rowsum(dx1)
    copies[0].wait()
    datt_ref[...] = nt(gx1, wo[...]).astype(BF)
    even = pair_masks(length)
    for seq in range(micro):
        allowed = allowed_of(segc_ref, segr_ref, seq, length)
        rows = slice(seq * length, (seq + 1) * length)
        for pair in range(HEADS // 2):
            lo = pair * 2 * HD
            queries = qkv_ref[rows, lo : lo + 2 * HD]
            key_stack = stacked(qkv_ref[rows, width + lo : width + lo + 2 * HD], even)
            value_stack = stacked(qkv_ref[rows, 2 * width + lo : 2 * width + lo + 2 * HD], even)
            probs = pair_probs(queries, key_stack, allowed, length)
            dmix = datt_ref[rows, lo : lo + 2 * HD]
            dprobs = nt(dmix, value_stack)
            low = []
            dscores = []
            for part in range(2):
                dp = dprobs[:, part * length : (part + 1) * length]
                inside = jnp.sum(probs[part] * dp, axis=-1, keepdims=True)
                ds = probs[part] * (dp - inside)
                dscores.append((ds * HD ** (-0.5)).astype(BF))
                low.append(probs[part].astype(BF))
            dq = nn(jnp.concatenate(dscores, axis=1), key_stack)
            dk = tn(jnp.concatenate(dscores, axis=0), stacked(queries, even))
            dv = tn(jnp.concatenate(low, axis=0), stacked(dmix, even))
            grads_ref[rows, lo : lo + 2 * HD] = dq.astype(BF)
            grads_ref[rows, width + lo : width + lo + 2 * HD] = dk.astype(BF)
            grads_ref[rows, 2 * width + lo : 2 * width + lo + 2 * HD] = dv.astype(BF)
    hat, scale = normalised(x_ref[...])
    copies[1].wait()
    da1 = jnp.zeros(dx1.shape, F32)
    for part in range(3):
        cols = slice(part * width, (part + 1) * width)
        piece = grads_ref[:, cols]
        if save:
            dbqkv[:, cols] = rowsum(piece.astype(F32))
        da1 = da1 + nt(piece, wqkv[:, cols])
    if save:
        dg1[...] = rowsum(da1 * hat)
        db1[...] = rowsum(da1)
        dx_ref[:, width:] = meta_ref[...]
    dx_ref[:, :width] = (dx1 + norm_back(da1, wide(g1), hat, scale)).astype(BF)


def att_back(dx1, hidden, qkv, seg_col, seg_row, gain, wqkv, wo, meta=None):
    save = meta is not None
    rows, width = dx1.shape
    span = qkv.shape[1]
    sds = jax.ShapeDtypeStruct
    if save:
        outs = [
            sds((rows, width + META), BF), sds((rows, span + width), BF), sds((1, width), F32),
            sds((1, width), F32), sds((1, span), F32), sds((1, width), F32),
        ]
        scratch = []
        extra, extra_specs = (meta,), [vmem_spec()]
    else:
        outs = [sds((rows, width), BF)]
        scratch = [pltpu.VMEM((rows, span), BF)]
        extra, extra_specs = (), []
    scratch = scratch + [
        pltpu.VMEM((rows, width), BF), pltpu.VMEM(wqkv.shape[1:], BF),
        pltpu.VMEM(wo.shape[1:], BF), pltpu.SemaphoreType.DMA((2,)),
    ]

    def kernel(*refs):
        att_back_kernel(*refs, save=save)

    return pl.pallas_call(
        kernel,
        out_shape=outs,
        in_specs=[vmem_spec()] * 6 + [any_spec()] * 2 + extra_specs,
        out_specs=[vmem_spec()] * len(outs),
        scratch_shapes=scratch,
        compiler_params=params(),
        name="att_back_save" if save else "att_back",
    )(dx1, hidden, qkv, seg_col, seg_row, gain, wqkv, wo, *extra)


def share_kernel(spots, wide_ref, mine_ref, theirs_ref, flat_ref, *, arrays, line):
    _, total = wide_ref.shape
    step = 2 * META
    for at in range(0, total, step):
        flat_ref[at : at + step, :] = wide_ref[:, at : at + step].T
    block = total // arrays // (4 * line)
    for slot in range(2):
        for array in range(arrays):
            for place in range(line):
                start = (array * line + spots[4 + place]) * 4 * block
                goal = ((slot * arrays + array) * line + place) * block
                for which, out in enumerate((mine_ref, theirs_ref)):
                    rows = pl.ds(pl.multiple_of(start + spots[2 * which + slot] * block, 16), block)
                    out[goal : goal + block, :] = flat_ref[rows, :]


def share(spots, saved, arrays, line):
    tokens, total = saved.shape
    block = total // arrays // (4 * line)
    if block % 16:
        flat = saved.T.reshape(arrays, line, 4, block, tokens)
        flat = jnp.take(flat, spots[4:], axis=1)
        picked = [lax.dynamic_index_in_dim(flat, spots[i], 2, keepdims=False) for i in range(4)]
        return (
            jnp.stack(picked[:2]).reshape(total // 2, tokens),
            jnp.stack(picked[2:]).reshape(total // 2, tokens),
        )
    out = jax.ShapeDtypeStruct((total // 2, tokens), BF)

    def kernel(*refs):
        share_kernel(*refs, arrays=arrays, line=line)

    return pl.pallas_call(
        kernel,
        out_shape=[out, out],
        in_specs=[smem_spec(), vmem_spec()],
        out_specs=[vmem_spec()] * 2,
        scratch_shapes=[pltpu.VMEM((total, tokens), BF)],
        compiler_params=params(),
    )(spots, saved)


def product(mine, theirs, grads, other, slot, parts, received=None):
    arrays = parts[0][1]
    rows = mine.shape[0] // (2 * arrays)
    cols = grads.shape[1]
    half = rows // 2

    def kernel(mine_ref, theirs_ref, grads_ref, other_ref, *rest):
        for array, _, at, size in parts:
            start = (slot * arrays + array) * rows
            for low in range(at, at + size, 768):
                these = slice(low, low + 768)
                value = nn(mine_ref[start : start + rows, :], grads_ref[:, these]) + nn(
                    theirs_ref[start : start + rows, :], other_ref[:, these]
                )
                if slot:
                    rest[0][:, these] = value.astype(BF)
                else:
                    value = value + rest[0][:, these].astype(F32)
                    rest[1][:, these] = value[:half]
                    rest[2][:, these] = value[half:].astype(BF)

    extra = () if slot else (received,)
    sds = jax.ShapeDtypeStruct
    outs = [sds((rows, cols), BF)] if slot else [sds((half, cols), F32), sds((half, cols), BF)]
    return pl.pallas_call(
        kernel,
        out_shape=outs,
        in_specs=[vmem_spec()] * (4 + len(extra)),
        out_specs=[vmem_spec()] * len(outs),
        compiler_params=params(),
    )(mine, theirs, grads, other, *extra)


def head_kernel(
    h_ref, tgt_ref, gain, offset, table_ref,
    dh_ref, ext_ref, dgain, doff, loss_ref,
    logits, top, total, picked, dhn, length,
):
    turn = pl.program_id(0)
    block = pl.program_id(1)
    blocks = pl.num_programs(1)
    rows, width = h_ref.shape
    size = table_ref.shape[0]

    @pl.when((turn == 0) & (block == 0))
    def _():
        hat, _ = normalised(h_ref[...])
        ext_ref[:, :width] = (hat * wide(gain) + wide(offset)).astype(BF)
        top[...] = jnp.full(top.shape, -1e30, F32)
        total[...] = jnp.zeros(total.shape, F32)
        picked[...] = jnp.zeros(picked.shape, F32)
        dhn[...] = jnp.zeros(dhn.shape, F32)

    words = block * size + lax.broadcasted_iota(jnp.int32, (rows, size), 1)
    hits = words == tgt_ref[...]

    @pl.when(turn == 0)
    def _():
        piece = nt(ext_ref[:, :width], table_ref[...])
        logits[block] = piece
        now = jnp.maximum(top[...], jnp.max(piece, axis=1, keepdims=True))
        total[...] = total[...] * jnp.exp(top[...] - now) + jnp.sum(
            jnp.exp(piece - now), axis=1, keepdims=True
        )
        top[...] = now
        picked[...] += jnp.sum(jnp.where(hits, piece, 0.0), axis=1, keepdims=True)

    @pl.when((turn == 1) & (block == 0))
    def _():
        top[...] = top[...] + jnp.log(total[...])
        lse = top[...]
        loss_ref[...] = jnp.sum(lse - picked[...], axis=0, keepdims=True) / length
        high = lse.astype(BF).astype(F32)
        mid = (lse - high).astype(BF).astype(F32)
        low = lse - high - mid
        tgt = tgt_ref[...]
        tgt_high = (tgt >> 8).astype(F32)
        tgt_low = (tgt & 255).astype(F32)
        lane = lax.broadcasted_iota(jnp.int32, (rows, META), 1)
        meta = jnp.zeros((rows, META), F32)
        for index, column in enumerate((high, mid, low, tgt_high, tgt_low)):
            meta = jnp.where(lane == index, column, meta)
        ext_ref[:, width:] = meta.astype(BF)

    @pl.when(turn == 1)
    def _():
        probs = jnp.exp(logits[block] - top[...])
        dlog = ((probs - hits.astype(F32)) / length).astype(BF)
        dhn[...] += nn(dlog, table_ref[...])

    @pl.when((turn == 1) & (block == blocks - 1))
    def _():
        hat, scale = normalised(h_ref[...])
        grad = dhn[...]
        dgain[...] = rowsum(grad * hat)
        doff[...] = rowsum(grad)
        dh_ref[...] = norm_back(grad, wide(gain), hat, scale)


def head(hidden, targets, gain, offset, table, length):
    rows, width = hidden.shape
    vocab = table.shape[0]
    size = math.gcd(vocab, 1024)
    blocks = vocab // size
    sds = jax.ShapeDtypeStruct

    def kernel(*refs):
        head_kernel(*refs, length=length)

    def full(shape):
        return pl.BlockSpec(shape, lambda t, b: (0,) * len(shape))

    outs = [
        sds((rows, width), F32), sds((rows, width + META), BF), sds((1, width), F32),
        sds((1, width), F32), sds((1, 1), F32),
    ]
    return pl.pallas_call(
        kernel,
        grid=(2, blocks),
        out_shape=outs,
        in_specs=[
            full((rows, width)), full((rows, 1)), full((1, width)), full((1, width)),
            pl.BlockSpec((size, width), lambda t, b: (b, 0)),
        ],
        out_specs=[full(out.shape) for out in outs],
        scratch_shapes=[
            pltpu.VMEM((blocks, rows, size), F32), pltpu.VMEM((rows, 1), F32),
            pltpu.VMEM((rows, 1), F32), pltpu.VMEM((rows, 1), F32),
            pltpu.VMEM((rows, width), F32),
        ],
        compiler_params=params(),
        name="head",
    )(hidden, targets, gain, offset, table)


def table_kernel(base_ref, ext_ref, shard_ref, out_ref, *, length):
    width = shard_ref.shape[1]
    size = shard_ref.shape[0]
    rows = ext_ref.shape[0]

    @pl.when(pl.program_id(0) == 0)
    def _():
        out_ref[...] = jnp.zeros(out_ref.shape, F32)

    hn = ext_ref[:, :width]
    meta = ext_ref[:, width:].astype(F32)
    lse = meta[:, 0:1] + meta[:, 1:2] + meta[:, 2:3]
    target = meta[:, 3:4] * 256.0 + meta[:, 4:5]
    words = (base_ref[0] + lax.broadcasted_iota(jnp.int32, (rows, size), 1)).astype(F32)
    probs = jnp.exp(nt(hn, shard_ref[...]) - lse)
    dlog = ((probs - (words == target).astype(F32)) / length).astype(BF)
    out_ref[...] += tn(dlog, hn)


def table_head(base, ext, shard, length):
    rows = ext.shape[0]
    step = math.gcd(rows, 512)
    width = shard.shape[1]

    def kernel(*refs):
        table_kernel(*refs, length=length)

    return pl.pallas_call(
        kernel,
        grid=(rows // step,),
        out_shape=jax.ShapeDtypeStruct(shard.shape, F32),
        in_specs=[
            pl.BlockSpec(memory_space=pltpu.SMEM),
            pl.BlockSpec((step, width + META), lambda r: (r, 0)),
            pl.BlockSpec(shard.shape, lambda r: (0, 0)),
        ],
        out_specs=pl.BlockSpec(shard.shape, lambda r: (0, 0)),
        compiler_params=params(),
        name="table_head",
    )(base, ext, shard)


def lookup_kernel(base_ref, ext_ref, table_out, pos_out):
    width = table_out.shape[1]
    rows = ext_ref.shape[0]

    @pl.when(pl.program_id(0) == 0)
    def _():
        table_out[...] = jnp.zeros(table_out.shape, F32)
        pos_out[...] = jnp.zeros(pos_out.shape, F32)

    dx = ext_ref[:, :width]
    meta = ext_ref[:, width:].astype(F32)
    token = meta[:, 0:1] * 256.0 + meta[:, 1:2]
    place = meta[:, 2:3] * 256.0 + meta[:, 3:4]
    for index, (value, out) in enumerate(((token, table_out), (place, pos_out))):
        size = out.shape[0]
        names = (base_ref[index] + lax.broadcasted_iota(jnp.int32, (rows, size), 1)).astype(F32)
        chosen = (names == value).astype(F32).astype(BF)
        out[...] += tn(chosen, dx)


def lookup_back(bases, ext, table_rows, pos_rows, width):
    rows = ext.shape[0]
    step = math.gcd(rows, 512)
    outs = [
        jax.ShapeDtypeStruct((table_rows, width), F32),
        jax.ShapeDtypeStruct((pos_rows, width), F32),
    ]
    return pl.pallas_call(
        lookup_kernel,
        grid=(rows // step,),
        out_shape=outs,
        in_specs=[
            pl.BlockSpec(memory_space=pltpu.SMEM),
            pl.BlockSpec((step, width + META), lambda r: (r, 0)),
        ],
        out_specs=[pl.BlockSpec(out.shape, lambda r: (0, 0)) for out in outs],
        compiler_params=params(),
        name="lookup_back",
    )(bases, ext)


class Line:
    def __init__(self):
        self.size = lax.axis_size("dp")
        self.line = self.size // 4
        self.index = lax.axis_index("dp")
        self.core = self.index % 2
        self.pair = (self.index // 2) % 2
        self.place = self.index // 4

    def swap(self, array, bit):
        return lax.ppermute(array, "dp", [(i, i ^ bit) for i in range(self.size)])

    def order(self):
        bits = self.line.bit_length() - 1
        turned = [int(format(k, "b").zfill(bits)[::-1], 2) if bits else 0 for k in range(self.line)]
        return [self.place ^ k for k in turned]

    def line_sum(self, kept, sent):
        bit = 1
        while bit < self.line:
            got = self.swap(sent, 4 * bit)
            bit *= 2
            if bit < self.line:
                half = kept.shape[0] // 2
                sent = (kept[half:] + got[half:].astype(F32)).astype(BF)
                kept = kept[:half] + got[:half].astype(F32)
            else:
                kept = kept + got.astype(F32)
        return kept


def body(
    token_ids, target_ids, segment_ids, token_embed, pos_embed, final_gain, final_bias,
    ln1_gain, ln1_bias, qkv_weight, qv_bias, out_weight, out_bias, ln2_gain, ln2_bias,
    fc_weight, fc_bias, proj_weight, proj_bias,
):
    on_first = lax.axis_index("section") == 0
    line = Line()
    micro, length = token_ids.shape
    rows = micro * length
    shard, width = token_embed.shape
    pos_shard = pos_embed.shape[0] // line.size

    full_table = lax.all_gather(token_embed, "dp", axis=0, tiled=True)
    earlier = segment_ids[:, None, :] < segment_ids[:, :, None]
    places = jnp.arange(length, dtype=jnp.int32)[None, :] - jnp.sum(
        earlier.astype(jnp.int32), axis=2
    )
    flat_places = places.reshape(-1)
    flat_ids = token_ids.reshape(-1)
    embedded = jnp.take(full_table, flat_ids, axis=0).astype(F32) + jnp.take(
        pos_embed, flat_places, axis=0
    ).astype(F32)

    seg_col = segment_ids.reshape(rows, 1)
    bqkv = jnp.concatenate(
        [qv_bias[:, :width], jnp.zeros((1, width), qv_bias.dtype), qv_bias[:, width:]], axis=1
    )
    vectors = (ln1_gain, ln1_bias, bqkv, out_bias, ln2_gain, ln2_bias, fc_bias, proj_bias)
    weights = (qkv_weight, out_weight, fc_weight, proj_weight)
    first = on_first.astype(jnp.int32).reshape(1)
    own = line.pair * 2
    other = 2 - own
    spots = jnp.stack(
        [own + line.core, other + line.core, own + 1 - line.core, other + 1 - line.core]
        + line.order()
    ).astype(jnp.int32)
    lane = jnp.arange(META, dtype=jnp.int32)[None, :]
    meta = jnp.zeros((rows, META), F32)
    for index, column in enumerate(
        (flat_ids >> 8, flat_ids & 255, flat_places >> 8, flat_places & 255)
    ):
        meta = jnp.where(lane == index, column.astype(F32)[:, None], meta)
    meta = meta.astype(BF)

    (first_out,) = forward_layer(embedded, seg_col, segment_ids, vectors, weights)
    incoming = lax.ppermute(first_out, "section", [(0, 1)])
    out, hidden, acts, qkv, x1, inner, act = forward_layer(
        embedded, seg_col, segment_ids, vectors, weights, incoming, first
    )
    dh, ext, dgain, doff, loss = head(
        out, target_ids.reshape(rows, 1), final_gain[None], final_bias[None], full_table, length
    )
    half = rows // 2
    ext_moved = lax.ppermute(ext[half:], "section", [(1, 0)])
    ext_own = jnp.where(on_first, ext_moved, ext[:half])
    ext_all = lax.all_gather(ext_own, "dp", axis=0, tiled=True)

    (mid,) = mlp_back(dh, x1, inner, ln2_gain, fc_weight, proj_weight)
    (back,) = att_back(mid, hidden, qkv, seg_col, segment_ids, ln1_gain, qkv_weight, out_weight)
    back_in = lax.ppermute(back, "section", [(1, 0)])

    mine_p, theirs_p = share(spots, act, 1, line.line)
    got_p = line.swap(theirs_p, 1)
    mine_a, theirs_a = share(spots, acts, 3, line.line)
    got_a = line.swap(theirs_a, 1)

    gy = jnp.where(on_first, back_in, dh.astype(BF))
    gy_other = line.swap(gy, 1)
    units = fc_weight.shape[2]
    span = qkv_weight.shape[2]
    proj_parts = ((0, 1, 0, width),)
    fc_parts = ((2, 3, 0, units),)
    att_parts = ((0, 3, 0, span), (1, 3, span, width))
    (proj_sent,) = product(mine_p, got_p, gy, gy_other, 1, proj_parts)
    proj_got = line.swap(proj_sent, 2)
    dx1, gin, dg2, db2, dfc, dproj = mlp_back(
        dh, x1, inner, ln2_gain, fc_weight, proj_weight, gy, first
    )
    gin_other = line.swap(gin, 1)
    (fc_sent,) = product(mine_a, got_a, gin, gin_other, 1, fc_parts)
    fc_got = line.swap(fc_sent, 2)
    dx_ext, grads, dg1, db1, dbqkv, dbo = att_back(
        dx1, hidden, qkv, seg_col, segment_ids, ln1_gain, qkv_weight, out_weight, meta
    )
    grads_other = line.swap(grads, 1)
    (att_sent,) = product(mine_a, got_a, grads, grads_other, 1, att_parts)
    att_got = line.swap(att_sent, 2)
    proj_own = product(mine_p, got_p, gy, gy_other, 0, proj_parts, proj_got)
    proj_share = line.line_sum(*proj_own)
    fc_own = product(mine_a, got_a, gin, gin_other, 0, fc_parts, fc_got)
    fc_share = line.line_sum(*fc_own)
    att_own = product(mine_a, got_a, grads, grads_other, 0, att_parts, att_got)
    att_share = line.line_sum(*att_own)
    qkv_share, out_share = att_share[:, :span], att_share[:, span:]

    base = line.index * shard
    table_part = table_head(base.reshape(1), ext_all, token_embed, length)

    dx_moved = lax.ppermute(dx_ext[half:], "section", [(0, 1)])
    dx_own = jnp.where(on_first, dx_ext[:half], dx_moved)
    dx_all = lax.all_gather(dx_own, "dp", axis=0, tiled=True)
    bases = jnp.stack([base, line.index * pos_shard])
    lookup, pos_part = lookup_back(bases, dx_all, shard, pos_shard, width)

    masked = [jnp.where(on_first, 0.0, v) for v in (dgain, doff)]
    small = [dg1, db1, dbqkv[:, :width], dbqkv[:, 2 * width :], dbo, dg2, db2, dfc, dproj]
    qv = jnp.concatenate(small[2:4], axis=1)
    small = [small[0], small[1], qv] + small[4:] + masked
    widths = [v.shape[1] // line.size for v in small]
    loss_own = jnp.where(on_first, 0.0, loss[0, 0])
    packed = jnp.concatenate(
        [v.reshape(line.size, -1) for v in small] + [jnp.full((line.size, 1), loss_own, F32)],
        axis=1,
    )
    spread = lax.all_to_all(packed, "dp", 0, 0, tiled=True)
    summed = jnp.sum(spread, axis=0)
    pieces = []
    at = 0
    for size in widths:
        pieces.append(summed[at : at + size])
        at += size
    tail = summed[sum(widths[:-2]) :]
    both = [(0, 1), (1, 0)]
    tail = tail + lax.ppermute(tail, "section", both)
    g_fin, b_fin = tail[: widths[-2]], tail[widths[-2] : widths[-2] + widths[-1]]
    loss_value = tail[-1] / (micro * line.size)
    table_sum = table_part + lax.ppermute(table_part, "section", both)
    late = jnp.concatenate([lookup, pos_part], axis=0)
    late = lax.reduce_precision(late, 8, 7)
    late = late + lax.ppermute(late.astype(BF), "section", both).astype(F32)
    table_sum = table_sum + late[:shard]
    pos_sum = late[shard:]
    return (
        loss_value, table_sum, pos_sum, g_fin, b_fin,
        pieces[0][None], pieces[1][None], qkv_share[None], pieces[2][None], out_share[None],
        pieces[3][None], pieces[4][None], pieces[5][None], fc_share[None], pieces[6][None],
        proj_share[None], pieces[7][None],
    )


def solution(mesh):
    in_specs = (
        P("dp", None), P("dp", None), P("dp", None), P("dp", None), P(), P(), P(),
        P("section", None), P("section", None), P("section", None, None), P("section", None),
        P("section", None, None), P("section", None), P("section", None), P("section", None),
        P("section", None, None), P("section", None), P("section", None, None), P("section", None),
    )
    out_specs = (
        P(), P("dp", None), P("dp", None), P("dp"), P("dp"),
        P("section", "dp"), P("section", "dp"), P("section", "dp", None), P("section", "dp"),
        P("section", "dp", None), P("section", "dp"), P("section", "dp"), P("section", "dp"),
        P("section", "dp", None), P("section", "dp"), P("section", "dp", None),
        P("section", "dp"),
    )
    return jax.shard_map(body, mesh=mesh, in_specs=in_specs, out_specs=out_specs, check_vma=False)
```

```python
import math

import jax
import jax.numpy as jnp
from jax import lax
from jax.experimental import pallas as pl
from jax.experimental.pallas import tpu as pltpu
from jax.sharding import PartitionSpec as P


HEADS = 12
HD = 64
BF = jnp.bfloat16
F32 = jnp.float32
META = 128
VMEM_LIMIT = 60 * 1024 * 1024


def nn(left, right):
    return lax.dot_general(left, right, (((1,), (0,)), ((), ())), preferred_element_type=F32)


def nt(left, right):
    return lax.dot_general(left, right, (((1,), (1,)), ((), ())), preferred_element_type=F32)


def tn(left, right):
    return lax.dot_general(left, right, (((0,), (0,)), ((), ())), preferred_element_type=F32)


def normalised(values):
    centre = jnp.mean(values, axis=-1, keepdims=True)
    shifted = values - centre
    spread = jnp.mean(shifted * shifted, axis=-1, keepdims=True)
    scale = lax.rsqrt(spread + 1e-05)
    return shifted * scale, scale


def norm_back(grad, gain, hat, scale):
    ghat = grad * gain
    first = jnp.mean(ghat, axis=-1, keepdims=True)
    second = jnp.mean(ghat * hat, axis=-1, keepdims=True)
    return scale * (ghat - first - hat * second)


def rowsum(values):
    return jnp.sum(values, axis=0, keepdims=True)


TANH_SCALE = math.sqrt(2.0 / math.pi)


def gelu_parts(inner):
    square = inner * inner
    bend = jnp.tanh(TANH_SCALE * (inner + 0.044715 * (square * inner)))
    return 0.5 * (1.0 + bend), bend, square


def pair_masks(length):
    lane = lax.broadcasted_iota(jnp.int32, (length, 2 * HD), 1)
    return lane < HD


def stacked(values, even):
    zero = jnp.zeros_like(values)
    return jnp.concatenate(
        [jnp.where(even, values, zero), jnp.where(even, zero, values)], axis=0
    )


def pair_probs(queries, key_stack, allowed, length):
    scores = nt(queries, key_stack) * HD ** (-0.5)
    probs = []
    for part in range(2):
        own = jnp.where(allowed, scores[:, part * length : (part + 1) * length], -1e30)
        peak = jnp.max(own, axis=-1, keepdims=True)
        raised = jnp.exp(own - peak)
        probs.append(raised * (1.0 / jnp.sum(raised, axis=-1, keepdims=True)))
    return probs


def allowed_of(segc_ref, segr_ref, seq, length):
    rows = lax.broadcasted_iota(jnp.int32, (length, length), 0)
    cols = lax.broadcasted_iota(jnp.int32, (length, length), 1)
    same = segc_ref[pl.ds(seq * length, length), :] == segr_ref[pl.ds(seq, 1), :]
    return (rows >= cols) & same


def start_copies(pairs, sems):
    copies = [pltpu.make_async_copy(src, dst, sems.at[i]) for i, (src, dst) in enumerate(pairs)]
    for copy in copies:
        copy.start()
    return copies


def forward_kernel(
    x_ref, segc_ref, segr_ref, g1, b1, bqkv, bo, g2, b2, bfc, bproj,
    wqkv_h, wo_h, wfc_h, wproj_h, *rest, save,
):
    width = x_ref.shape[1]
    if save:
        come_ref, first, y_ref, hid_ref, acts_ref, qkv_ref, x1_ref, inner_ref, act_ref = rest[:9]
        att_at = width
        wqkv, wo, wfc, wproj, sems = rest[9:]
    else:
        y_ref, qkv_ref, acts_ref, wqkv, wo, wfc, wproj, sems = rest
        att_at = 0
    copies = start_copies(
        ((wqkv_h.at[0], wqkv), (wo_h.at[0], wo), (wfc_h.at[0], wfc), (wproj_h.at[0], wproj)), sems
    )
    micro, length = segr_ref.shape
    hidden = x_ref[...]
    if save:
        hidden = jnp.where(first[0] == 1, hidden, come_ref[...].astype(F32))
        hid_ref[...] = hidden
    hat, _ = normalised(hidden)
    a1 = (hat * wide(g1) + wide(b1)).astype(BF)
    if save:
        acts_ref[:, :width] = a1
    copies[0].wait()
    for part in range(3):
        cols = slice(part * width, (part + 1) * width)
        qkv_ref[:, cols] = (nn(a1, wqkv[:, cols]) + bqkv[:, cols].astype(F32)).astype(BF)
    even = pair_masks(length)
    for seq in range(micro):
        allowed = allowed_of(segc_ref, segr_ref, seq, length)
        rows = slice(seq * length, (seq + 1) * length)
        for pair in range(HEADS // 2):
            lo = pair * 2 * HD
            queries = qkv_ref[rows, lo : lo + 2 * HD]
            key_stack = stacked(qkv_ref[rows, width + lo : width + lo + 2 * HD], even)
            value_stack = stacked(qkv_ref[rows, 2 * width + lo : 2 * width + lo + 2 * HD], even)
            probs = pair_probs(queries, key_stack, allowed, length)
            joined = jnp.concatenate([part.astype(BF) for part in probs], axis=1)
            acts_ref[rows, att_at + lo : att_at + lo + 2 * HD] = nn(joined, value_stack).astype(BF)
    copies[1].wait()
    x1 = hidden + nn(acts_ref[:, att_at : att_at + width], wo[...]) + wide(bo)
    hat2, _ = normalised(x1)
    a2 = (hat2 * wide(g2) + wide(b2)).astype(BF)
    if save:
        x1_ref[...] = x1
        acts_ref[:, 2 * width :] = a2
    copies[2].wait()
    copies[3].wait()
    total = x1 + wide(bproj)
    hidden_units = wfc.shape[1]
    for part in range(hidden_units // width):
        cols = slice(part * width, (part + 1) * width)
        inner = nn(a2, wfc[:, cols]) + bfc[:, cols].astype(F32)
        half, _, _ = gelu_parts(inner)
        act = (inner * half).astype(BF)
        if save:
            inner_ref[:, cols] = inner
            act_ref[:, cols] = act
        total = total + nn(act, wproj[cols, :])
    y_ref[...] = total.astype(y_ref.dtype)


def wide(ref):
    return ref[...].astype(F32)


def any_spec():
    return pl.BlockSpec(memory_space=pl.ANY)


def vmem_spec():
    return pl.BlockSpec(memory_space=pltpu.VMEM)


def smem_spec():
    return pl.BlockSpec(memory_space=pltpu.SMEM)


def params():
    return pltpu.CompilerParams(vmem_limit_bytes=VMEM_LIMIT)


def forward_layer(hidden, seg_col, seg_row, vectors, weights, incoming=None, first=None):
    save = incoming is not None
    rows, width = hidden.shape
    units = weights[2].shape[2]
    span = weights[0].shape[2]
    sds = jax.ShapeDtypeStruct
    if save:
        outs = [
            sds((rows, width), F32), sds((rows, width), F32), sds((rows, 3 * width), BF),
            sds((rows, span), BF), sds((rows, width), F32), sds((rows, units), F32),
            sds((rows, units), BF),
        ]
        scratch = []
        extra, extra_specs = (incoming, first), [vmem_spec(), smem_spec()]
    else:
        outs = [sds((rows, width), BF)]
        scratch = [pltpu.VMEM((rows, span), BF), pltpu.VMEM((rows, width), BF)]
        extra, extra_specs = (), []
    scratch = scratch + [pltpu.VMEM(w.shape[1:], BF) for w in weights]
    scratch.append(pltpu.SemaphoreType.DMA((4,)))

    def kernel(*refs):
        forward_kernel(*refs, save=save)

    return pl.pallas_call(
        kernel,
        out_shape=outs,
        in_specs=[vmem_spec()] * 11 + [any_spec()] * 4 + extra_specs,
        out_specs=[vmem_spec()] * len(outs),
        scratch_shapes=scratch,
        compiler_params=params(),
        name="fwd2" if save else "fwd1",
    )(hidden, seg_col, seg_row, *vectors, *weights, *extra)


def mlp_back_kernel(dy_ref, x1_ref, inner_ref, g2, wfc_h, wproj_h, *rest, save):
    if save:
        gy_ref, first, dx1_ref, gin_ref, dg2, db2, dfc, dproj, wfc, wproj, sems = rest
    else:
        dx1_ref, wfc, wproj, sems = rest
    width = dy_ref.shape[1]
    units = inner_ref.shape[1]
    pieces = []
    for low in range(0, units, width):
        these = slice(low, low + width)
        pieces += [(wproj_h.at[0, these, :], wproj.at[these, :])]
        pieces += [(wfc_h.at[0, :, these], wfc.at[:, these])]
    copies = start_copies(pieces, sems)
    dy = dy_ref[...]
    if save:
        gy = gy_ref[...]
        dy = jnp.where(first[0] == 1, gy.astype(F32), dy)
        dproj[...] = rowsum(dy)
    else:
        gy = dy.astype(BF)
    hat, scale = normalised(x1_ref[...])
    da2 = jnp.zeros(dy.shape, F32)
    for part in range(units // width):
        cols = slice(part * width, (part + 1) * width)
        copies[2 * part].wait()
        dact = nt(gy, wproj[cols, :])
        inner = inner_ref[:, cols]
        half, bend, square = gelu_parts(inner)
        slope = half + (0.5 * TANH_SCALE) * inner * (1.0 - bend * bend) * (
            1.0 + (3 * 0.044715) * square
        )
        gin = (dact * slope).astype(BF)
        if save:
            gin_ref[:, cols] = gin
            dfc[:, cols] = rowsum(gin.astype(F32))
        copies[2 * part + 1].wait()
        da2 = da2 + nt(gin, wfc[:, cols])
    if save:
        dg2[...] = rowsum(da2 * hat)
        db2[...] = rowsum(da2)
    dx1_ref[...] = dy + norm_back(da2, wide(g2), hat, scale)


def mlp_back(dy, x1, inner, gain, wfc, wproj, gy=None, first=None):
    save = gy is not None
    rows, width = dy.shape
    units = inner.shape[1]
    sds = jax.ShapeDtypeStruct
    outs = [sds((rows, width), F32)]
    extra, extra_specs = (), []
    if save:
        outs += [
            sds((rows, units), BF), sds((1, width), F32), sds((1, width), F32),
            sds((1, units), F32), sds((1, width), F32),
        ]
        extra, extra_specs = (gy, first), [vmem_spec(), smem_spec()]

    def kernel(*refs):
        mlp_back_kernel(*refs, save=save)

    return pl.pallas_call(
        kernel,
        out_shape=outs,
        in_specs=[vmem_spec()] * 4 + [any_spec()] * 2 + extra_specs,
        out_specs=[vmem_spec()] * len(outs),
        scratch_shapes=[
            pltpu.VMEM(wfc.shape[1:], BF), pltpu.VMEM(wproj.shape[1:], BF),
            pltpu.SemaphoreType.DMA((2 * (units // width),)),
        ],
        compiler_params=params(),
        name="mlp2" if save else "mlp1",
    )(dy, x1, inner, gain, wfc, wproj, *extra)


def att_back_kernel(dx1_ref, x_ref, qkv_ref, segc_ref, segr_ref, g1, wqkv_h, wo_h, *rest, save):
    if save:
        meta_ref, dx_ref, grads_ref, dg1, db1, dbqkv, dbo, datt_ref, wqkv, wo, sems = rest
    else:
        dx_ref, grads_ref, datt_ref, wqkv, wo, sems = rest
    copies = start_copies(((wo_h.at[0], wo), (wqkv_h.at[0], wqkv)), sems)
    micro, length = segr_ref.shape
    width = x_ref.shape[1]
    dx1 = dx1_ref[...]
    gx1 = dx1.astype(BF)
    if save:
        grads_ref[:, 3 * width :] = gx1
        dbo[...] = rowsum(dx1)
    copies[0].wait()
    datt_ref[...] = nt(gx1, wo[...]).astype(BF)
    even = pair_masks(length)
    for seq in range(micro):
        allowed = allowed_of(segc_ref, segr_ref, seq, length)
        rows = slice(seq * length, (seq + 1) * length)
        for pair in range(HEADS // 2):
            lo = pair * 2 * HD
            queries = qkv_ref[rows, lo : lo + 2 * HD]
            key_stack = stacked(qkv_ref[rows, width + lo : width + lo + 2 * HD], even)
            value_stack = stacked(qkv_ref[rows, 2 * width + lo : 2 * width + lo + 2 * HD], even)
            probs = pair_probs(queries, key_stack, allowed, length)
            dmix = datt_ref[rows, lo : lo + 2 * HD]
            dprobs = nt(dmix, value_stack)
            low = []
            dscores = []
            for part in range(2):
                dp = dprobs[:, part * length : (part + 1) * length]
                inside = jnp.sum(probs[part] * dp, axis=-1, keepdims=True)
                ds = probs[part] * (dp - inside)
                dscores.append((ds * HD ** (-0.5)).astype(BF))
                low.append(probs[part].astype(BF))
            dq = nn(jnp.concatenate(dscores, axis=1), key_stack)
            dk = tn(jnp.concatenate(dscores, axis=0), stacked(queries, even))
            dv = tn(jnp.concatenate(low, axis=0), stacked(dmix, even))
            grads_ref[rows, lo : lo + 2 * HD] = dq.astype(BF)
            grads_ref[rows, width + lo : width + lo + 2 * HD] = dk.astype(BF)
            grads_ref[rows, 2 * width + lo : 2 * width + lo + 2 * HD] = dv.astype(BF)
    hat, scale = normalised(x_ref[...])
    copies[1].wait()
    da1 = jnp.zeros(dx1.shape, F32)
    for part in range(3):
        cols = slice(part * width, (part + 1) * width)
        piece = grads_ref[:, cols]
        if save:
            dbqkv[:, cols] = rowsum(piece.astype(F32))
        da1 = da1 + nt(piece, wqkv[:, cols])
    if save:
        dg1[...] = rowsum(da1 * hat)
        db1[...] = rowsum(da1)
        dx_ref[:, width:] = meta_ref[...]
    dx_ref[:, :width] = (dx1 + norm_back(da1, wide(g1), hat, scale)).astype(BF)


def att_back(dx1, hidden, qkv, seg_col, seg_row, gain, wqkv, wo, meta=None):
    save = meta is not None
    rows, width = dx1.shape
    span = qkv.shape[1]
    sds = jax.ShapeDtypeStruct
    if save:
        outs = [
            sds((rows, width + META), BF), sds((rows, span + width), BF), sds((1, width), F32),
            sds((1, width), F32), sds((1, span), F32), sds((1, width), F32),
        ]
        scratch = []
        extra, extra_specs = (meta,), [vmem_spec()]
    else:
        outs = [sds((rows, width), BF)]
        scratch = [pltpu.VMEM((rows, span), BF)]
        extra, extra_specs = (), []
    scratch = scratch + [
        pltpu.VMEM((rows, width), BF), pltpu.VMEM(wqkv.shape[1:], BF),
        pltpu.VMEM(wo.shape[1:], BF), pltpu.SemaphoreType.DMA((2,)),
    ]

    def kernel(*refs):
        att_back_kernel(*refs, save=save)

    return pl.pallas_call(
        kernel,
        out_shape=outs,
        in_specs=[vmem_spec()] * 6 + [any_spec()] * 2 + extra_specs,
        out_specs=[vmem_spec()] * len(outs),
        scratch_shapes=scratch,
        compiler_params=params(),
        name="att2" if save else "att1",
    )(dx1, hidden, qkv, seg_col, seg_row, gain, wqkv, wo, *extra)


def share_kernel(spots, wide_ref, mine_ref, theirs_ref, flat_ref, *, arrays, line):
    _, total = wide_ref.shape
    step = 2 * META
    for at in range(0, total, step):
        flat_ref[at : at + step, :] = wide_ref[:, at : at + step].T
    block = total // arrays // (4 * line)
    for slot in range(2):
        for array in range(arrays):
            for place in range(line):
                start = (array * line + spots[4 + place]) * 4 * block
                goal = ((slot * arrays + array) * line + place) * block
                for which, out in enumerate((mine_ref, theirs_ref)):
                    rows = pl.ds(pl.multiple_of(start + spots[2 * which + slot] * block, 16), block)
                    out[goal : goal + block, :] = flat_ref[rows, :]


def share(spots, saved, arrays, line):
    tokens, total = saved.shape
    block = total // arrays // (4 * line)
    if block % 16:
        flat = saved.T.reshape(arrays, line, 4, block, tokens)
        flat = jnp.take(flat, spots[4:], axis=1)
        picked = [lax.dynamic_index_in_dim(flat, spots[i], 2, keepdims=False) for i in range(4)]
        return (
            jnp.stack(picked[:2]).reshape(total // 2, tokens),
            jnp.stack(picked[2:]).reshape(total // 2, tokens),
        )
    out = jax.ShapeDtypeStruct((total // 2, tokens), BF)

    def kernel(*refs):
        share_kernel(*refs, arrays=arrays, line=line)

    return pl.pallas_call(
        kernel,
        out_shape=[out, out],
        in_specs=[smem_spec(), vmem_spec()],
        out_specs=[vmem_spec()] * 2,
        scratch_shapes=[pltpu.VMEM((total, tokens), BF)],
        compiler_params=params(),
    )(spots, saved)


def product(mine, theirs, grads, other, slot, parts, received=None):
    arrays = parts[0][1]
    rows = mine.shape[0] // (2 * arrays)
    cols = grads.shape[1]
    half = rows // 2

    def kernel(mine_ref, theirs_ref, grads_ref, other_ref, *rest):
        for array, _, at, size in parts:
            start = (slot * arrays + array) * rows
            for low in range(at, at + size, 768):
                these = slice(low, low + 768)
                value = nn(mine_ref[start : start + rows, :], grads_ref[:, these]) + nn(
                    theirs_ref[start : start + rows, :], other_ref[:, these]
                )
                if slot:
                    rest[0][:, these] = value.astype(BF)
                else:
                    value = value + rest[0][:, these].astype(F32)
                    rest[1][:, these] = value[:half]
                    rest[2][:, these] = value[half:].astype(BF)

    extra = () if slot else (received,)
    sds = jax.ShapeDtypeStruct
    outs = [sds((rows, cols), BF)] if slot else [sds((half, cols), F32), sds((half, cols), BF)]
    return pl.pallas_call(
        kernel,
        out_shape=outs,
        in_specs=[vmem_spec()] * (4 + len(extra)),
        out_specs=[vmem_spec()] * len(outs),
        compiler_params=params(),
    )(mine, theirs, grads, other, *extra)


def head_kernel(
    h_ref, tgt_ref, gain, offset, table_ref,
    dh_ref, ext_ref, dgain, doff, loss_ref,
    logits, top, total, picked, dhn, length,
):
    turn = pl.program_id(0)
    block = pl.program_id(1)
    blocks = pl.num_programs(1)
    rows, width = h_ref.shape
    size = table_ref.shape[0]

    @pl.when((turn == 0) & (block == 0))
    def _():
        hat, _ = normalised(h_ref[...])
        ext_ref[:, :width] = (hat * wide(gain) + wide(offset)).astype(BF)
        top[...] = jnp.full(top.shape, -1e30, F32)
        total[...] = jnp.zeros(total.shape, F32)
        picked[...] = jnp.zeros(picked.shape, F32)
        dhn[...] = jnp.zeros(dhn.shape, F32)

    words = block * size + lax.broadcasted_iota(jnp.int32, (rows, size), 1)
    hits = words == tgt_ref[...]

    @pl.when(turn == 0)
    def _():
        piece = nt(ext_ref[:, :width], table_ref[...])
        logits[block] = piece
        now = jnp.maximum(top[...], jnp.max(piece, axis=1, keepdims=True))
        total[...] = total[...] * jnp.exp(top[...] - now) + jnp.sum(
            jnp.exp(piece - now), axis=1, keepdims=True
        )
        top[...] = now
        picked[...] += jnp.sum(jnp.where(hits, piece, 0.0), axis=1, keepdims=True)

    @pl.when((turn == 1) & (block == 0))
    def _():
        top[...] = top[...] + jnp.log(total[...])
        lse = top[...]
        loss_ref[...] = jnp.sum(lse - picked[...], axis=0, keepdims=True) / length
        high = lse.astype(BF).astype(F32)
        mid = (lse - high).astype(BF).astype(F32)
        low = lse - high - mid
        tgt = tgt_ref[...]
        tgt_high = (tgt >> 8).astype(F32)
        tgt_low = (tgt & 255).astype(F32)
        lane = lax.broadcasted_iota(jnp.int32, (rows, META), 1)
        meta = jnp.zeros((rows, META), F32)
        for index, column in enumerate((high, mid, low, tgt_high, tgt_low)):
            meta = jnp.where(lane == index, column, meta)
        ext_ref[:, width:] = meta.astype(BF)

    @pl.when(turn == 1)
    def _():
        probs = jnp.exp(logits[block] - top[...])
        dlog = ((probs - hits.astype(F32)) / length).astype(BF)
        dhn[...] += nn(dlog, table_ref[...])

    @pl.when((turn == 1) & (block == blocks - 1))
    def _():
        hat, scale = normalised(h_ref[...])
        grad = dhn[...]
        dgain[...] = rowsum(grad * hat)
        doff[...] = rowsum(grad)
        dh_ref[...] = norm_back(grad, wide(gain), hat, scale)


def head(hidden, targets, gain, offset, table, length):
    rows, width = hidden.shape
    vocab = table.shape[0]
    size = math.gcd(vocab, 1024)
    blocks = vocab // size
    sds = jax.ShapeDtypeStruct

    def kernel(*refs):
        head_kernel(*refs, length=length)

    def full(shape):
        return pl.BlockSpec(shape, lambda t, b: (0,) * len(shape))

    outs = [
        sds((rows, width), F32), sds((rows, width + META), BF), sds((1, width), F32),
        sds((1, width), F32), sds((1, 1), F32),
    ]
    return pl.pallas_call(
        kernel,
        grid=(2, blocks),
        out_shape=outs,
        in_specs=[
            full((rows, width)), full((rows, 1)), full((1, width)), full((1, width)),
            pl.BlockSpec((size, width), lambda t, b: (b, 0)),
        ],
        out_specs=[full(out.shape) for out in outs],
        scratch_shapes=[
            pltpu.VMEM((blocks, rows, size), F32), pltpu.VMEM((rows, 1), F32),
            pltpu.VMEM((rows, 1), F32), pltpu.VMEM((rows, 1), F32),
            pltpu.VMEM((rows, width), F32),
        ],
        compiler_params=params(),
        name="head",
    )(hidden, targets, gain, offset, table)


def table_kernel(base_ref, ext_ref, shard_ref, out_ref, *, length):
    width = shard_ref.shape[1]
    size = shard_ref.shape[0]
    rows = ext_ref.shape[0]

    @pl.when(pl.program_id(0) == 0)
    def _():
        out_ref[...] = jnp.zeros(out_ref.shape, F32)

    hn = ext_ref[:, :width]
    meta = ext_ref[:, width:].astype(F32)
    lse = meta[:, 0:1] + meta[:, 1:2] + meta[:, 2:3]
    target = meta[:, 3:4] * 256.0 + meta[:, 4:5]
    words = (base_ref[0] + lax.broadcasted_iota(jnp.int32, (rows, size), 1)).astype(F32)
    probs = jnp.exp(nt(hn, shard_ref[...]) - lse)
    dlog = ((probs - (words == target).astype(F32)) / length).astype(BF)
    out_ref[...] += tn(dlog, hn)


def table_head(base, ext, shard, length):
    rows = ext.shape[0]
    step = math.gcd(rows, 512)
    width = shard.shape[1]

    def kernel(*refs):
        table_kernel(*refs, length=length)

    return pl.pallas_call(
        kernel,
        grid=(rows // step,),
        out_shape=jax.ShapeDtypeStruct(shard.shape, F32),
        in_specs=[
            pl.BlockSpec(memory_space=pltpu.SMEM),
            pl.BlockSpec((step, width + META), lambda r: (r, 0)),
            pl.BlockSpec(shard.shape, lambda r: (0, 0)),
        ],
        out_specs=pl.BlockSpec(shard.shape, lambda r: (0, 0)),
        compiler_params=params(),
        name="thead",
    )(base, ext, shard)


def lookup_kernel(base_ref, ext_ref, table_out, pos_out):
    width = table_out.shape[1]
    rows = ext_ref.shape[0]

    @pl.when(pl.program_id(0) == 0)
    def _():
        table_out[...] = jnp.zeros(table_out.shape, F32)
        pos_out[...] = jnp.zeros(pos_out.shape, F32)

    dx = ext_ref[:, :width]
    meta = ext_ref[:, width:].astype(F32)
    token = meta[:, 0:1] * 256.0 + meta[:, 1:2]
    place = meta[:, 2:3] * 256.0 + meta[:, 3:4]
    for index, (value, out) in enumerate(((token, table_out), (place, pos_out))):
        size = out.shape[0]
        names = (base_ref[index] + lax.broadcasted_iota(jnp.int32, (rows, size), 1)).astype(F32)
        chosen = (names == value).astype(F32).astype(BF)
        out[...] += tn(chosen, dx)


def lookup_back(bases, ext, table_rows, pos_rows, width):
    rows = ext.shape[0]
    step = math.gcd(rows, 512)
    outs = [
        jax.ShapeDtypeStruct((table_rows, width), F32),
        jax.ShapeDtypeStruct((pos_rows, width), F32),
    ]
    return pl.pallas_call(
        lookup_kernel,
        grid=(rows // step,),
        out_shape=outs,
        in_specs=[
            pl.BlockSpec(memory_space=pltpu.SMEM),
            pl.BlockSpec((step, width + META), lambda r: (r, 0)),
        ],
        out_specs=[pl.BlockSpec(out.shape, lambda r: (0, 0)) for out in outs],
        compiler_params=params(),
        name="look",
    )(bases, ext)


class Line:
    def __init__(self):
        self.size = lax.axis_size("dp")
        self.line = self.size // 4
        self.index = lax.axis_index("dp")
        self.core = self.index % 2
        self.pair = (self.index // 2) % 2
        self.place = self.index // 4

    def swap(self, array, bit):
        return lax.ppermute(array, "dp", [(i, i ^ bit) for i in range(self.size)])

    def order(self):
        bits = self.line.bit_length() - 1
        turned = [
            sum(((k >> i) & 1) << (bits - 1 - i) for i in range(bits)) for k in range(self.line)
        ]
        return [self.place ^ k for k in turned]

    def line_sum(self, kept, sent):
        bit = 1
        while bit < self.line:
            got = self.swap(sent, 4 * bit)
            bit *= 2
            if bit < self.line:
                half = kept.shape[0] // 2
                sent = (kept[half:] + got[half:].astype(F32)).astype(BF)
                kept = kept[:half] + got[:half].astype(F32)
            else:
                kept = kept + got.astype(F32)
        return kept


def body(
    token_ids, target_ids, segment_ids, token_embed, pos_embed, final_gain, final_bias,
    ln1_gain, ln1_bias, qkv_weight, qv_bias, out_weight, out_bias, ln2_gain, ln2_bias,
    fc_weight, fc_bias, proj_weight, proj_bias,
):
    on_first = lax.axis_index("section") == 0
    line = Line()
    micro, length = token_ids.shape
    rows = micro * length
    shard, width = token_embed.shape
    pos_shard = pos_embed.shape[0] // line.size

    full_table = lax.all_gather(token_embed, "dp", axis=0, tiled=True)
    earlier = segment_ids[:, None, :] < segment_ids[:, :, None]
    places = jnp.arange(length, dtype=jnp.int32)[None, :] - jnp.sum(
        earlier.astype(jnp.int32), axis=2
    )
    flat_places = places.reshape(-1)
    flat_ids = token_ids.reshape(-1)
    embedded = jnp.take(full_table, flat_ids, axis=0).astype(F32) + jnp.take(
        pos_embed, flat_places, axis=0
    ).astype(F32)

    seg_col = segment_ids.reshape(rows, 1)
    bqkv = jnp.concatenate(
        [qv_bias[:, :width], jnp.zeros((1, width), qv_bias.dtype), qv_bias[:, width:]], axis=1
    )
    vectors = (ln1_gain, ln1_bias, bqkv, out_bias, ln2_gain, ln2_bias, fc_bias, proj_bias)
    weights = (qkv_weight, out_weight, fc_weight, proj_weight)
    first = on_first.astype(jnp.int32).reshape(1)
    own = line.pair * 2
    other = 2 - own
    spots = jnp.stack(
        [own + line.core, other + line.core, own + 1 - line.core, other + 1 - line.core]
        + line.order()
    ).astype(jnp.int32)
    lane = jnp.arange(META, dtype=jnp.int32)[None, :]
    meta = jnp.zeros((rows, META), F32)
    for index, column in enumerate(
        (flat_ids >> 8, flat_ids & 255, flat_places >> 8, flat_places & 255)
    ):
        meta = jnp.where(lane == index, column.astype(F32)[:, None], meta)
    meta = meta.astype(BF)

    (first_out,) = forward_layer(embedded, seg_col, segment_ids, vectors, weights)
    incoming = lax.ppermute(first_out, "section", [(0, 1)])
    out, hidden, acts, qkv, x1, inner, act = forward_layer(
        embedded, seg_col, segment_ids, vectors, weights, incoming, first
    )
    dh, ext, dgain, doff, loss = head(
        out, target_ids.reshape(rows, 1), final_gain[None], final_bias[None], full_table, length
    )
    half = rows // 2
    ext_moved = lax.ppermute(ext[half:], "section", [(1, 0)])
    ext_own = jnp.where(on_first, ext_moved, ext[:half])
    ext_all = lax.all_gather(ext_own, "dp", axis=0, tiled=True)

    (mid,) = mlp_back(dh, x1, inner, ln2_gain, fc_weight, proj_weight)
    (back,) = att_back(mid, hidden, qkv, seg_col, segment_ids, ln1_gain, qkv_weight, out_weight)
    back_in = lax.ppermute(back, "section", [(1, 0)])

    mine_p, theirs_p = share(spots, act, 1, line.line)
    got_p = line.swap(theirs_p, 1)
    mine_a, theirs_a = share(spots, acts, 3, line.line)
    got_a = line.swap(theirs_a, 1)

    gy = jnp.where(on_first, back_in, dh.astype(BF))
    gy_other = line.swap(gy, 1)
    units = fc_weight.shape[2]
    span = qkv_weight.shape[2]
    proj_parts = ((0, 1, 0, width),)
    fc_parts = ((2, 3, 0, units),)
    att_parts = ((0, 3, 0, span), (1, 3, span, width))
    (proj_sent,) = product(mine_p, got_p, gy, gy_other, 1, proj_parts)
    proj_got = line.swap(proj_sent, 2)
    dx1, gin, dg2, db2, dfc, dproj = mlp_back(
        dh, x1, inner, ln2_gain, fc_weight, proj_weight, gy, first
    )
    gin_other = line.swap(gin, 1)
    (fc_sent,) = product(mine_a, got_a, gin, gin_other, 1, fc_parts)
    fc_got = line.swap(fc_sent, 2)
    dx_ext, grads, dg1, db1, dbqkv, dbo = att_back(
        dx1, hidden, qkv, seg_col, segment_ids, ln1_gain, qkv_weight, out_weight, meta
    )
    grads_other = line.swap(grads, 1)
    (att_sent,) = product(mine_a, got_a, grads, grads_other, 1, att_parts)
    att_got = line.swap(att_sent, 2)
    proj_own = product(mine_p, got_p, gy, gy_other, 0, proj_parts, proj_got)
    proj_share = line.line_sum(*proj_own)
    fc_own = product(mine_a, got_a, gin, gin_other, 0, fc_parts, fc_got)
    fc_share = line.line_sum(*fc_own)
    att_own = product(mine_a, got_a, grads, grads_other, 0, att_parts, att_got)
    att_share = line.line_sum(*att_own)
    qkv_share, out_share = att_share[:, :span], att_share[:, span:]

    base = line.index * shard
    table_part = table_head(base.reshape(1), ext_all, token_embed, length)

    dx_moved = lax.ppermute(dx_ext[half:], "section", [(0, 1)])
    dx_own = jnp.where(on_first, dx_ext[:half], dx_moved)
    dx_all = lax.all_gather(dx_own, "dp", axis=0, tiled=True)
    bases = jnp.stack([base, line.index * pos_shard])
    lookup, pos_part = lookup_back(bases, dx_all, shard, pos_shard, width)

    masked = [jnp.where(on_first, 0.0, v) for v in (dgain, doff)]
    small = [dg1, db1, dbqkv[:, :width], dbqkv[:, 2 * width :], dbo, dg2, db2, dfc, dproj]
    qv = jnp.concatenate(small[2:4], axis=1)
    small = [small[0], small[1], qv] + small[4:] + masked
    widths = [v.shape[1] // line.size for v in small]
    loss_own = jnp.where(on_first, 0.0, loss[0, 0])
    packed = jnp.concatenate(
        [v.reshape(line.size, -1) for v in small] + [jnp.full((line.size, 1), loss_own, F32)],
        axis=1,
    )
    spread = lax.all_to_all(packed, "dp", 0, 0, tiled=True)
    summed = jnp.sum(spread, axis=0)
    pieces = []
    at = 0
    for size in widths:
        pieces.append(summed[at : at + size])
        at += size
    tail = summed[sum(widths[:-2]) :]
    both = [(0, 1), (1, 0)]
    tail = tail + lax.ppermute(tail, "section", both)
    g_fin, b_fin = tail[: widths[-2]], tail[widths[-2] : widths[-2] + widths[-1]]
    loss_value = tail[-1] / (micro * line.size)
    table_sum = table_part + lax.ppermute(table_part, "section", both)
    late = jnp.concatenate([lookup, pos_part], axis=0)
    late = lax.reduce_precision(late, 8, 7)
    late = late + lax.ppermute(late.astype(BF), "section", both).astype(F32)
    table_sum = table_sum + late[:shard]
    pos_sum = late[shard:]
    return (
        loss_value, table_sum, pos_sum, g_fin, b_fin,
        pieces[0][None], pieces[1][None], qkv_share[None], pieces[2][None], out_share[None],
        pieces[3][None], pieces[4][None], pieces[5][None], fc_share[None], pieces[6][None],
        proj_share[None], pieces[7][None],
    )


def solution(mesh):
    in_specs = (
        P("dp", None), P("dp", None), P("dp", None), P("dp", None), P(), P(), P(),
        P("section", None), P("section", None), P("section", None, None), P("section", None),
        P("section", None, None), P("section", None), P("section", None), P("section", None),
        P("section", None, None), P("section", None), P("section", None, None), P("section", None),
    )
    out_specs = (
        P(), P("dp", None), P("dp", None), P("dp"), P("dp"),
        P("section", "dp"), P("section", "dp"), P("section", "dp", None), P("section", "dp"),
        P("section", "dp", None), P("section", "dp"), P("section", "dp"), P("section", "dp"),
        P("section", "dp", None), P("section", "dp"), P("section", "dp", None),
        P("section", "dp"),
    )
    return jax.shard_map(body, mesh=mesh, in_specs=in_specs, out_specs=out_specs, check_vma=False)
```
